512 devices in a mesh: gx: 32 (over y, x), gy: 16 (over z, core).
Axes of the slice: x: 4, y: 8, z: 8, core: 2. Of those that a mesh axis runs over, the one named last changes fastest.
Arguments:
- rhs: float32 [8, 512, 2048], P(None, 'gx', 'gy'), may hold values from -6 to 6
- cond_class: int32 [8, 512, 2048], P(None, 'gx', 'gy'), may hold values from 0 to 15
- charge_class: int32 [8, 512, 2048], P(None, 'gx', 'gy'), may hold values from 0 to 15
- cond_table: float32 [16], replicated, may hold values from 0.1 to 1
- charge_table: float32 [16], replicated, may hold values from 0 to 0.5
Outputs:
- correction: float32 [8, 512, 2048], P(None, 'gx', 'gy')
- residual: float32 [8, 512, 2048], P(None, 'gx', 'gy')
The draws below stay inside these ranges and needn't reach their ends.
All inputs are finite; a program needn't handle non-finite values.
Results may differ from the reference program's by a relative error of at most 0.0003.
Values sent between devices are 32-bit elements; how exact they have to be, the bound alone decides.
A program may use at most 64 MiB of HBM per device.

```python
import math
import jax
import jax.numpy as jnp
from jax import lax

LAYERS = 8
LEVELS = 4
PRE_SWEEPS = 2
POST_SWEEPS = 2
COARSE_SWEEPS = 6
CYCLES = 2
NCLASS = 16
NX = 512
NY = 2048


def draw_rhs(key, part):
    shape = (LAYERS, NX, NY)
    return jax.random.truncated_normal(key, -6.0, 6.0, shape, jnp.float32)


def with_ends(drawn, key, least, largest):
    shape = drawn.shape
    place = [jax.random.randint(jax.random.fold_in(key, axis), (), 0, shape[axis]) for axis in range(len(shape))]
    drawn = drawn.at[tuple(place)].set(least)
    longest = shape.index(max(shape))
    place[longest] = (place[longest] + 1) % shape[longest]
    return drawn.at[tuple(place)].set(largest)


def setup_inputs(seed: int = 0) -> dict:
    arg_keys = jax.random.split(jax.random.key(seed), 6)
    rhs = draw_rhs(jax.random.fold_in(arg_keys[5], 71), 0)
    cond_class = with_ends(jax.random.randint(arg_keys[1], (LAYERS, NX, NY), 0, NCLASS), jax.random.fold_in(arg_keys[1], 1), 0, NCLASS - 1).astype(jnp.int32)
    charge_class = with_ends(jax.random.randint(arg_keys[2], (LAYERS, NX, NY), 0, NCLASS), jax.random.fold_in(arg_keys[2], 1), 0, NCLASS - 1).astype(jnp.int32)
    cond_table = jnp.clip(jnp.exp(jax.random.uniform(arg_keys[3], (NCLASS,), jnp.float32, math.log(0.1), math.log(1.0))), 0.1, 1.0)
    charge_table = jnp.clip(jax.random.uniform(arg_keys[4], (NCLASS,), jnp.float32, 0.0, 0.5), 0.0, 0.5)
    return dict(rhs=rhs, cond_class=cond_class, charge_class=charge_class, cond_table=cond_table, charge_table=charge_table)


relax_weight = 0.9
shift_weight = 0.1


def blur_along(padded, along):
    extent = padded.shape[along] - 2
    lower_side = lax.slice_in_dim(padded, 0, extent, axis=along)
    middle = lax.slice_in_dim(padded, 1, extent + 1, axis=along)
    upper_side = lax.slice_in_dim(padded, 2, extent + 2, axis=along)
    return 0.5 * lower_side + middle + 0.5 * upper_side


def blur_cells(padded):
    along_y = blur_along(padded, 3)
    along_x = blur_along(along_y, 2)
    deeper = jnp.pad(along_x, ((0, 0), (1, 1), (0, 0), (0, 0)))
    return blur_along(deeper, 1)


def plain_rims(stacked):
    return jnp.pad(stacked, ((0, 0), (0, 0), (1, 1), (1, 1)))


def coarsen(field):
    depth_cells, width_x, width_y = field.shape
    blocks = field.reshape(depth_cells // 2, 2, width_x // 2, 2, width_y // 2, 2)
    return jnp.mean(blocks, axis=(1, 3, 5))


def refine(field):
    depth_cells, width_x, width_y = field.shape
    copies = jnp.broadcast_to(field[:, None, :, None, :, None], (depth_cells, 2, width_x, 2, width_y, 2))
    return copies.reshape(2 * depth_cells, 2 * width_x, 2 * width_y)


def diagonal_of(conduct, factor, padder):
    blurred = blur_cells(padder(conduct[None]))[0]
    beside_all = 2.0 * blurred - 2.0 * conduct
    return factor * 0.5 * (14.0 * conduct + beside_all) + shift_weight * conduct


def operate(iterate, conduct, diagonal, factor, padder):
    flux_term = conduct * iterate
    blurred = blur_cells(padder(jnp.stack([iterate, flux_term])))
    near_iterate = 2.0 * blurred[0] - 2.0 * iterate
    near_flux = 2.0 * blurred[1] - 2.0 * flux_term
    return diagonal * iterate - factor * 0.5 * (conduct * near_iterate + near_flux)


def smooth(iterate, source, conduct, diagonal, factor, padder, sweeps):
    for repeat in range(sweeps):
        iterate = iterate + relax_weight * (source - operate(iterate, conduct, diagonal, factor, padder)) / diagonal
    return iterate


def smooth_from_zero(source, conduct, diagonal, factor, padder, sweeps):
    iterate = relax_weight * source / diagonal
    return smooth(iterate, source, conduct, diagonal, factor, padder, sweeps - 1)


def reference(rhs, cond_class, charge_class, cond_table, charge_table):
    conduct = cond_table[cond_class] * (1.0 - charge_table[charge_class])
    conducts = [conduct]
    for grid_level in range(1, LEVELS):
        conducts.append(coarsen(conducts[-1]))
    factors = [0.25 ** grid_level for grid_level in range(LEVELS)]
    diagonals = [diagonal_of(conducts[grid_level], factors[grid_level], plain_rims) for grid_level in range(LEVELS)]
    last_level = LEVELS - 1

    def vcycle(grid_level, source):
        here_conduct = conducts[grid_level]
        here_diagonal = diagonals[grid_level]
        factor = factors[grid_level]
        if grid_level == last_level:
            return smooth_from_zero(source, here_conduct, here_diagonal, factor, plain_rims, COARSE_SWEEPS)
        iterate = smooth_from_zero(source, here_conduct, here_diagonal, factor, plain_rims, PRE_SWEEPS)
        remainder = source - operate(iterate, here_conduct, here_diagonal, factor, plain_rims)
        iterate = iterate + refine(vcycle(grid_level + 1, coarsen(remainder)))
        return smooth(iterate, source, here_conduct, here_diagonal, factor, plain_rims, POST_SWEEPS)

    correction = jnp.zeros_like(rhs)
    residual = rhs
    for repeat in range(CYCLES):
        correction = correction + vcycle(0, residual)
        residual = rhs - operate(correction, conducts[0], diagonals[0], factors[0], plain_rims)
    return correction, residual
```

```python
import functools

import jax
import jax.numpy as jnp
from jax import lax
from jax.experimental import pallas as pl
from jax.experimental.pallas import tpu as pltpu
from jax.sharding import PartitionSpec as P

MESH = pl.DeviceIdType.MESH
CYCLES = 2
COARSE_SWEEPS = 6
RELAX = 0.9
SHIFT = 0.1
DEPTH, WIDE, LONG = 8, 16, 128
REACH = (-4, -3, -2, -1, 1, 2, 3, 4)
SIDES = ((1, 0), (-1, 0), (0, 1), (0, -1), (1, 1), (1, -1), (-1, 1), (-1, -1))

FINE, MID, SHORT, FAR = 0, 24, 48, 54
COPIES = 78


def roll(x, shift, axis):
    shift %= x.shape[axis]
    return pltpu.roll(x, shift, axis) if shift else x


def pick(x, index):
    return jnp.take_along_axis(x, index, axis=1)


def blur(fields):
    along = []
    for v in fields:
        y = v + 0.5 * (roll(v, 1, 1) + roll(v, -1, 1))
        along.append(y + 0.5 * (roll(y, 1, 0) + roll(y, -1, 0)))
    out = []
    for d, v in enumerate(along):
        beside = [along[e] for e in (d - 1, d + 1) if 0 <= e < len(along)]
        out.append(v + 0.5 * functools.reduce(jnp.add, beside) if beside else v)
    return out


def operate(v, c, big):
    spread = blur(v)
    flux = blur([a * b for a, b in zip(c, v)])
    return [g * a - (b * s + f) for g, a, b, s, f in zip(big, v, c, spread, flux)]


def sweep(v, f, c, w, big):
    return [a + q * (s - o) for a, q, s, o in zip(v, w, f, operate(v, c, big))]


def residual_of(v, f, c, big):
    return [s - o for s, o in zip(f, operate(v, c, big))]


def diagonal(c, level):
    shift = SHIFT * 4.0**level
    return [(6.0 + shift) * a + b for a, b in zip(c, blur(c))]


def weight(c, diag):
    return [jnp.where(a > 0.0, RELAX / jnp.where(a > 0.0, d, 1.0), 0.0) for a, d in zip(c, diag)]


def look_up(classes, table):
    bits = [(classes & (1 << b)) != 0 for b in range(4)]
    level = [table[i] for i in range(16)]
    for bit in bits:
        level = [jnp.where(bit, level[2 * i + 1], level[2 * i]) for i in range(len(level) // 2)]
    return level[0]


def kernel(gx_count, gy_count, rhs, cond, charge, cond_table, charge_table, out, res, *scratch):
    (C, W, D, F, VA, VB, K, PS, PR, T, C1, W1, D1, F1, X1, V1, R1, E1, G, S2, AS, AR, BS, BR, C2, W2, D2, F2, V2, G3, H2, H1,
     Z, send_sem, recv_sem) = scratch
    gx, gy = lax.axis_index("gx"), lax.axis_index("gy")

    def at(dx, dy):
        return (lax.rem(gx + (dx + gx_count), gx_count), lax.rem(gy + (dy + gy_count), gy_count))

    def copy(src, dst, number, where):
        return pltpu.make_async_remote_copy(
            src_ref=src, dst_ref=dst, send_sem=send_sem.at[number], recv_sem=recv_sem.at[number],
            device_id=where, device_id_type=MESH,
        )

    left_in, right_in = gy > 0, gy < gy_count - 1
    low_in = jnp.where(gx > 0, 1.0, 0.0)
    high_in = jnp.where(gx < gx_count - 1, 1.0, 0.0)
    lane = lax.broadcasted_iota(jnp.int32, (8, 128), 1)
    sub = lax.broadcasted_iota(jnp.int32, (8, 128), 0)
    lane24 = lax.broadcasted_iota(jnp.int32, (24, 128), 1)
    first, last = lane == 0, lane == 127
    above = jnp.where(sub == 0, 0.0, 0.5)
    below = jnp.where(sub == 7, 0.0, 0.5)
    yes_left = jnp.where(left_in, 1.0, 0.0)
    yes_right = jnp.where(right_in, 1.0, 0.0)


    def fine_copies(n, array, h):
        ends = (
            (array.at[0, pl.ds(24 - h, h)], array.at[0, pl.ds(8 - h, h)]),
            (array.at[0, pl.ds(8, h)], array.at[0, pl.ds(24, h)]),
            (PS.at[n], PR.at[n, 0, pl.ds(1, 2)]),
            (PS.at[n], PR.at[n, 1, pl.ds(1, 2)]),
            (PS.at[n, 1], PR.at[n, 0, 0]),
            (PS.at[n, 1], PR.at[n, 1, 0]),
            (PS.at[n, 0], PR.at[n, 0, 3]),
            (PS.at[n, 0], PR.at[n, 1, 3]),
        )
        return [copy(a, b, FINE + 8 * n + i, at(*SIDES[i])) for i, (a, b) in enumerate(ends)]

    def pack_edges(n, array):
        for b in range(2):
            packed = None
            for i in range(8):
                row = roll(array[0, 8 + 8 * b + i], 16 * i + 8, 1)
                packed = row if packed is None else jnp.where(lane >= 16 * i, row, packed)
            PS[n, b] = packed

    def unpack_edges(n, array, lo, hi):
        from_left = lax.rem(lane, 16) < 8
        for b in range(4):
            packed = jnp.where(from_left, PR[n, 0, b], PR[n, 1, b])
            for i in range(8):
                if lo <= 8 * b + i < hi:
                    array[1, 8 * b + i] = roll(packed, -(16 * i + 8), 1)

    def blur_row(t0, t1):
        a0, a1, b0, b1 = roll(t0, 1, 1), roll(t1, 1, 1), roll(t0, -1, 1), roll(t1, -1, 1)
        y0 = t0 + 0.5 * (jnp.where(first, a1, a0) + jnp.where(last, b1, b0))
        y1 = t1 + 0.5 * (jnp.where(first, a0, a1) + jnp.where(last, b0, b1))
        return [y + (above * roll(y, 1, 0) + below * roll(y, -1, 0)) for y in (y0, y1)]

    def blur_rows(row, lo, hi, use, flux=True):
        window = {}
        for r in range(lo - 1, hi + 1):
            v = row(r)
            fields = [v, [C[t, r] * v[t] for t in range(2)]] if flux else [v]
            window[r] = [blur_row(*f) for f in fields]
            q = r - 1
            if q >= lo:
                spread = [
                    [window[q][k][t] + 0.5 * (window[q - 1][k][t] + window[r][k][t]) for t in range(2)]
                    for k in range(len(fields))
                ]
                use(q, *spread)
                del window[q - 1]

    def fine_change(q, t, v, f, spread, flux):
        return f[t, q] - (D[t, q] * v - (C[t, q] * spread[t] + flux[t]))

    def fine_sweep(source, row, lo, hi, keep):
        def use(q, spread, flux):
            v = row(q)
            for t in range(2):
                keep(t, q, v[t] + W[t, q] * fine_change(q, t, v[t], source, spread, flux))

        blur_rows(row, lo, hi, use)

    def rows_of(array):
        return lambda r: [array[0, r], array[1, r]]

    def put(array):
        def keep(t, q, v):
            array[t, q] = v

        return keep

    def fine_pairs(t):
        return [T[t, pl.ds(2 * d, 24, stride=8), :] + T[t, pl.ds(2 * d + 1, 24, stride=8), :] for d in range(4)]

    twice = lax.rem(2 * lane24, 128)

    def along_pairs(v, index):
        return pick(v + roll(v, -1, 1), index)


    def mid_copies(n, source):
        return [copy(source, R1.at[n, i], MID + 8 * n + i, at(*SIDES[i])) for i in range(8)]

    def mid_whole(n, own):
        parts = []
        for middle, before, after in ((0, 4, 5), (None, 2, 3), (1, 6, 7)):
            rows = []
            for d in range(4):
                m = own[d] if middle is None else R1[n, middle, d]
                outer = jnp.where(lane < 32, R1[n, after, d], R1[n, before, d])
                rows.append(jnp.where(lane < 64, m, roll(outer, 64, 1)))
            parts.append(rows)
        return parts

    def pack2(a, b):
        return jnp.where(sub < 4, a, roll(b, 4, 0))

    spot = 2 * lax.rem(lane + 16, 32)

    def short_copies(n, count):
        k = n if n == 0 else n + 1
        src = AS.at[pl.ds(k, count)]
        return [copy(src, AR.at[s, pl.ds(k, count)], SHORT + 2 * n + s, at(0, (1, -1)[s])) for s in range(2)]

    def far_copies(n, count):
        k = n if n == 0 else n + 1
        src = BS.at[pl.ds(k, count)]
        return [
            copy(src, BR.at[4 - o, pl.ds(k, count)], FAR + 8 * n + i, at(o, 0)) for i, o in enumerate(REACH)
        ]

    def join_sides(k):
        left, right = AR[0, k], AR[1, k]
        return jnp.where(lane < 16, left, jnp.where(lane < 48, AS[k], right))

    def spread_far(k, array, mask):
        for g in range(5):
            pair = []
            for b in (2 * g, 2 * g + 1):
                block = BS[k] if b == 4 else jnp.zeros((8, 128), jnp.float32) if b == 9 else BR[b, k]
                if mask and b not in (4, 9):
                    there = jnp.where(jnp.logical_and(gx + (b - 4) >= 0, gx + (b - 4) < gx_count), 1.0, 0.0)
                    block = block * there
                pair.append(block)
            array[0, 8 * g : 8 * g + 8, :] = pack2(pair[0], pair[1])
            array[1, 8 * g : 8 * g + 8, :] = jnp.where(sub < 4, roll(pair[0], 4, 0), pair[1])

    def load(ref, count):
        return [ref[d] for d in range(count)]

    started = []

    def start(copies):
        for c in copies:
            c.start()
        started.extend(copies)
        return copies

    def arrive(copies):
        for c in copies:
            c.wait_recv()

    barrier = pltpu.get_barrier_semaphore()
    peers = list(SIDES) + [(o, 0) for o in REACH if abs(o) > 1]
    for peer in peers:
        pl.semaphore_signal(barrier, inc=1, device_id=at(*peer), device_id_type=MESH)

    for x in range(WIDE):
        where = pl.ds(x, DEPTH, stride=WIDE)
        F[0, 0, 8 + x] = rhs[where, :]
        C[0, 8 + x] = look_up(cond[where, :], cond_table) * (1.0 - look_up(charge[where, :], charge_table))
    pack_edges(0, C)
    pack_edges(1, F.at[0])
    T[...] = jnp.zeros_like(T)
    G[...] = jnp.zeros_like(G)
    G3[...] = jnp.zeros_like(G3)
    for q in range(8, 16):
        r = 2 * (q - 4)
        T[0, 8 * q : 8 * q + 8, :] = C[0, r] + C[0, r + 1]
    for d, v in enumerate(fine_pairs(0)):
        E1[d] = along_pairs(v, twice)[8:16] * (0.125 * 0.25)

    pl.semaphore_wait(barrier, len(peers))
    to_c = start(fine_copies(0, C, 7))
    to_f = start(fine_copies(1, F.at[0], 6))
    to_c1 = start(mid_copies(0, E1))

    arrive(to_c)
    unpack_edges(0, C, 1, 31)
    side = jnp.where(lane < 64, yes_right, yes_left)
    for r in range(1, 31):
        if r < 8 or r >= 24:
            mask = low_in if r < 8 else high_in
            C[0, r] = C[0, r] * mask
            C[1, r] = C[1, r] * (side * mask)
        else:
            C[1, r] = C[1, r] * side

    def coefficients(q, spread):
        for t in range(2):
            c = C[t, q]
            diag = (6.0 + SHIFT) * c + spread[t]
            inside = c > 0.0
            D[t, q] = diag + 2.0 * c
            W[t, q] = jnp.where(inside, RELAX / jnp.where(inside, diag, 1.0), 0.0)

    blur_rows(rows_of(C), 2, 30, coefficients, flux=False)

    for cycle in range(CYCLES):
        source = F.at[cycle]
        arrive(to_f)
        unpack_edges(1 + cycle, source, 2, 30)

        fine_sweep(source, lambda r: [W[t, r] * source[t, r] for t in range(2)], 3, 29, put(VB))
        held = {}

        def pair_up(q, spread, flux):
            v = [VB[0, q], VB[1, q]]
            for t in range(2):
                change = fine_change(q, t, v[t], source, spread, flux)
                if q % 2 == 0:
                    held[t] = change
                else:
                    at_row = 8 * (4 + q // 2)
                    T[t, at_row : at_row + 8, :] = held[t] + change

        blur_rows(rows_of(VB), 4, 28, pair_up)
        for d, (v0, v1) in enumerate(zip(fine_pairs(0), fine_pairs(1))):
            F1[cycle, d] = jnp.where(lane24 < 64, along_pairs(v0, twice), along_pairs(v1, twice)) * 0.125

        if cycle == 0:
            arrive(to_c1)
            whole = mid_whole(0, load(E1, 4))
            side = jnp.where(lane < 64, 1.0, jnp.where(lane < 96, yes_right, yes_left))
            for g, mask in enumerate((side * low_in, side, side * high_in)):
                for d in range(4):
                    C1[d, 8 * g : 8 * g + 8, :] = whole[g][d] * mask
            c1 = load(C1, 4)
            diag = diagonal(c1, 1)
            for d, w in enumerate(weight(c1, diag)):
                W1[d] = w
                D1[d] = diag[d] + 2.0 * c1[d]
            for d in range(2):
                G[d, 0:24, :] = c1[2 * d] + c1[2 * d + 1]
            c2 = []
            own = []
            for d in range(2):
                pairs = G[d, pl.ds(0, 16, stride=2), :] + G[d, pl.ds(1, 16, stride=2), :]
                c2.append(along_pairs(pairs, twice[:16]) * (0.125 * 0.25))
                pairs = G[d, pl.ds(8, 8, stride=2), :] + G[d, pl.ds(9, 8, stride=2), :]
                own.append(along_pairs(pairs, spot) * (0.125 * 0.25))
            AS[0] = pack2(own[0], own[1])
            own = []
            for d, v in enumerate(diagonal(c2, 2)):
                S2[d] = v
                own.append(pick(S2[d, 4:12, :], spot // 2))
            AS[1] = pack2(own[0], own[1])
            to_near_c = start(short_copies(0, 2))

        c1, w1, big1 = load(C1, 4), load(W1, 4), load(D1, 4)
        f1 = [F1[cycle, d] for d in range(4)]
        v1 = sweep([w * f for w, f in zip(w1, f1)], f1, c1, w1, big1)
        r1 = residual_of(v1, f1, c1, big1)
        own = []
        for d in range(2):
            G[d, 0:24, :] = r1[2 * d] + r1[2 * d + 1]
            pairs = G[d, pl.ds(8, 8, stride=2), :] + G[d, pl.ds(9, 8, stride=2), :]
            own.append(along_pairs(pairs, spot) * 0.125)
        k = 2 + cycle
        AS[k] = pack2(own[0], own[1])
        to_near = start(short_copies(1 + cycle, 1))
        to_f1 = start(mid_copies(1 + cycle, F1.at[cycle, :, pl.ds(8, 8), :]))

        if cycle == 0:
            arrive(to_near_c)
            side = jnp.where(lane < 16, yes_left, jnp.where(lane < 48, 1.0, yes_right))
            for j in range(2):
                BS[j] = join_sides(j) * side
            to_far_c = start(far_copies(0, 2))
        arrive(to_near)
        BS[k] = join_sides(k)
        to_far = start(far_copies(1 + cycle, 1))

        arrive(to_f1)
        whole = mid_whole(1 + cycle, [F1[cycle, d, 8:16, :] for d in range(4)])
        for g in range(3):
            for d in range(4):
                X1[d, 8 * g : 8 * g + 8, :] = whole[g][d]
        f1 = load(X1, 4)
        for d, v in enumerate(sweep([w * f for w, f in zip(w1, f1)], f1, c1, w1, big1)):
            V1[d] = v
        if cycle == 0:
            arrive(to_far_c)
            spread_far(0, C2, True)
            spread_far(1, D2, False)
            c2 = load(C2, 2)
            diag = load(D2, 2)
            for d, w in enumerate(weight(c2, diag)):
                W2[d] = w
                D2[d] = diag[d] + 2.0 * c2[d]
            G3[0:40, :] = c2[0] + c2[1]
            pairs = G3[pl.ds(0, 24, stride=2), :] + G3[pl.ds(1, 24, stride=2), :]
            c3 = [along_pairs(pairs, twice) * (0.125 * 0.25)]
            diag = diagonal(c3, 3)
            w3 = weight(c3, diag)
            big3 = [diag[0] + 2.0 * c3[0]]
            for j, v in enumerate((c3, w3, big3)):
                Z[j] = v[0]

        arrive(to_far)
        spread_far(k, F2, False)
        c2, w2, big2, f2 = load(C2, 2), load(W2, 2), load(D2, 2), load(F2, 2)
        v2 = sweep([w * f for w, f in zip(w2, f2)], f2, c2, w2, big2)
        for d in range(2):
            V2[d] = v2[d]
        r2 = residual_of(v2, f2, c2, big2)
        G3[0:40, :] = r2[0] + r2[1]

        pairs = G3[pl.ds(0, 24, stride=2), :] + G3[pl.ds(1, 24, stride=2), :]
        f3 = [along_pairs(pairs, twice) * 0.125]
        c3, w3, big3 = [Z[0]], [Z[1]], [Z[2]]
        v3 = [w3[0] * f3[0]]
        for _ in range(COARSE_SWEEPS - 1):
            v3 = sweep(v3, f3, c3, w3, big3)
        half = lane24 // 2
        up = pick(v3[0], half)
        H2[0, pl.ds(0, 24, stride=2), :] = up
        H2[0, pl.ds(1, 24, stride=2), :] = up

        c2, w2, big2, f2 = [[ref[d, 8:32, :] for d in range(2)] for ref in (C2, W2, D2, F2)]
        v2 = [V2[d, 8:32, :] + H2[0, 8:32, :] for d in range(2)]
        for _ in range(2):
            v2 = sweep(v2, f2, c2, w2, big2)
        down = jnp.where(lane24 < 96, 16 + half, half - 48)
        for d in range(2):
            up = pick(v2[d], down)
            H1[d, pl.ds(0, 24, stride=2), :] = up
            H1[d, pl.ds(1, 24, stride=2), :] = up

        c1, w1, big1, f1 = load(C1, 4), load(W1, 4), load(D1, 4), load(X1, 4)
        v1 = [V1[d] + H1[d // 2, 8:32, :] for d in range(4)]
        for _ in range(2):
            v1 = sweep(v1, f1, c1, w1, big1)
        for d in range(8):
            T[0, pl.ds(d, 24, stride=8), :] = v1[d // 2]

        near = lane // 2
        for q in range(6, 18):
            row = T[0, 8 * q : 8 * q + 8, :]
            up = [pick(row, near), pick(row, 64 + near)]
            for r in (2 * q - 8, 2 * q - 7):
                for t in range(2):
                    VA[t, r] = VB[t, r] + up[t]
        fine_sweep(source, rows_of(VA), 6, 26, put(VB))

        def add(t, q, v):
            K[t, q] = v if cycle == 0 else K[t, q] + v

        fine_sweep(source, rows_of(VB), 7, 25, add)

        def keep_residual(q, spread, flux):
            v = K[0, q]
            change = fine_change(q, 0, v, F.at[0], spread, flux)
            if cycle + 1 < CYCLES:
                F[cycle + 1, 0, q] = change
            else:
                res[pl.ds(q - 8, DEPTH, stride=WIDE), :] = change
                out[pl.ds(q - 8, DEPTH, stride=WIDE), :] = v

        blur_rows(rows_of(K), 8, 24, keep_residual)
        if cycle + 1 < CYCLES:
            pack_edges(2 + cycle, F.at[cycle + 1])
            to_f = start(fine_copies(2 + cycle, F.at[cycle + 1], 6))

    for c in started:
        c.wait_send()


def per_device(gx_count, gy_count, rhs, cond_class, charge_class, cond_table, charge_table):
    flat = (DEPTH * WIDE, LONG)
    f32 = jnp.float32
    tile = (8, 128)
    fine = pltpu.VMEM((2, 32) + tile, f32)
    mid = pltpu.VMEM((4, 24, 128), f32)
    low = pltpu.VMEM((2, 40, 128), f32)
    scratch = [
        fine, fine, fine, pltpu.VMEM((CYCLES, 2, 32) + tile, f32), fine, fine, fine,
        pltpu.VMEM((3, 2) + tile, f32), pltpu.VMEM((3, 2, 4) + tile, f32), pltpu.VMEM((2, 192, 128), f32),
        mid, mid, mid, pltpu.VMEM((CYCLES, 4, 24, 128), f32), mid, mid,
        pltpu.VMEM((3, 8, 4) + tile, f32), pltpu.VMEM((4,) + tile, f32),
        pltpu.VMEM((2, 32, 128), f32), pltpu.VMEM((2, 16, 128), f32),
        pltpu.VMEM((4,) + tile, f32), pltpu.VMEM((2, 4) + tile, f32),
        pltpu.VMEM((4,) + tile, f32), pltpu.VMEM((9, 4) + tile, f32),
        low, low, low, low, low, pltpu.VMEM((48, 128), f32),
        pltpu.VMEM((1, 48, 128), f32), pltpu.VMEM((2, 48, 128), f32), pltpu.VMEM((3, 24, 128), f32),
        pltpu.SemaphoreType.DMA((COPIES,)), pltpu.SemaphoreType.DMA((COPIES,)),
    ]
    vmem, smem = pl.BlockSpec(memory_space=pltpu.VMEM), pl.BlockSpec(memory_space=pltpu.SMEM)
    correction, residual = pl.pallas_call(
        functools.partial(kernel, gx_count, gy_count),
        out_shape=[jax.ShapeDtypeStruct(flat, f32)] * 2,
        in_specs=[vmem, vmem, vmem, smem, smem],
        out_specs=[vmem, vmem],
        scratch_shapes=scratch,
        compiler_params=pltpu.CompilerParams(collective_id=0, has_side_effects=True),
    )(rhs.reshape(flat), cond_class.reshape(flat), charge_class.reshape(flat), cond_table, charge_table)
    return correction.reshape(rhs.shape), residual.reshape(rhs.shape)


def solution(mesh):
    placed = (P(None, "gx", "gy"), P(None, "gx", "gy"), P(None, "gx", "gy"), P(), P())
    return jax.shard_map(
        functools.partial(per_device, mesh.shape["gx"], mesh.shape["gy"]),
        mesh=mesh,
        in_specs=placed,
        out_specs=(P(None, "gx", "gy"), P(None, "gx", "gy")),
        check_vma=False,
    )
```

```python
import functools

import jax
import jax.numpy as jnp
from jax import lax
from jax.experimental import pallas as pl
from jax.experimental.pallas import tpu as pltpu
from jax.sharding import PartitionSpec as P

MESH = pl.DeviceIdType.MESH
CYCLES = 2
COARSE_SWEEPS = 6
RELAX = 0.9
SHIFT = 0.1
DEPTH, WIDE, LONG = 8, 16, 128
OWN = 12
SIDES = ((1, 0), (-1, 0), (0, 1), (0, -1), (1, 1), (1, -1), (-1, 1), (-1, -1))
AROUND = tuple((a, b) for a in range(-5, 6) for b in (-1, 0, 1) if (a, b) != (0, 0))
NEARER = tuple(p for p in AROUND if abs(p[0]) < 5)

FINE, FINE_MORE, MID, FAR = 0, 16, 28, 31
COPIES = 34


def roll(x, shift, axis):
    shift %= x.shape[axis]
    return pltpu.roll(x, shift, axis) if shift else x


def pick(x, index):
    return jnp.take_along_axis(x, index, axis=1)


def blur(fields):
    along = []
    for v in fields:
        y = (v + v) + (roll(v, 1, 1) + roll(v, -1, 1))
        along.append((y + y) + (roll(y, 1, 0) + roll(y, -1, 0)))
    if len(along) == 1:
        return along
    pairs = [along[0]] + [a + b for a, b in zip(along, along[1:])] + [along[-1]]
    return [a + b for a, b in zip(pairs, pairs[1:])]


def operate(v, c, big):
    spread = blur(v)
    flux = blur([a * b for a, b in zip(c, v)])
    return [g * a - (b * s + f) for g, a, b, s, f in zip(big, v, c, spread, flux)]


def sweep(v, f, c, w, big):
    return [a + q * (s - o) for a, q, s, o in zip(v, w, f, operate(v, c, big))]


def residual_of(v, f, c, big):
    return [s - o for s, o in zip(f, operate(v, c, big))]


def diagonal(c, level, scale):
    own = scale * (6.0 + SHIFT * 4.0**level)
    return [own * a + b for a, b in zip(c, blur(c))]


def weight(c, diag):
    return [jnp.where(a > 0.0, RELAX / jnp.where(a > 0.0, d, 1.0), 0.0) for a, d in zip(c, diag)]


def look_up(classes, table):
    bits = [(classes & (1 << b)) != 0 for b in range(4)]
    level = [table[i] for i in range(16)]
    for bit in bits:
        level = [jnp.where(bit, level[2 * i + 1], level[2 * i]) for i in range(len(level) // 2)]
    return level[0]


def kernel(gx_count, gy_count, rhs_in, cond_in, charge_in, cond_table_in, charge_table_in, out, res, *scratch):
    (rhs, cond, charge, cond_table, charge_table, C, W, D, F, VA, VB, K, PS, PR, T, C1, W1, D1, F1, V1, E1, R1, E2, R2, G, S2,
     AS, BC, BF, BL, C2, W2, D2, F2, V2, G3, H2, H1, Z, send_sem, recv_sem, in_sem) = scratch
    gx, gy = lax.axis_index("gx"), lax.axis_index("gy")

    def at(dx, dy):
        return (lax.rem(gx + (dx + gx_count), gx_count), lax.rem(gy + (dy + gy_count), gy_count))

    def copy(src, dst, number, where):
        return pltpu.make_async_remote_copy(
            src_ref=src, dst_ref=dst, send_sem=send_sem.at[number], recv_sem=recv_sem.at[number],
            device_id=where, device_id_type=MESH,
        )

    barrier = pltpu.get_barrier_semaphore()
    for peer in AROUND:
        pl.semaphore_signal(barrier, inc=1, device_id=at(*peer), device_id_type=MESH)
    pairs = ((cond_table_in, cond_table), (charge_table_in, charge_table), (cond_in, cond), (charge_in, charge), (rhs_in, rhs))
    inputs = [pltpu.make_async_copy(a, b, in_sem.at[i]) for i, (a, b) in enumerate(pairs)]
    for c in inputs:
        c.start()

    left_in, right_in = gy > 0, gy < gy_count - 1
    low_in = jnp.where(gx > 0, 1.0, 0.0)
    high_in = jnp.where(gx < gx_count - 1, 1.0, 0.0)
    lane = lax.broadcasted_iota(jnp.int32, (8, 128), 1)
    sub = lax.broadcasted_iota(jnp.int32, (8, 128), 0)
    lane24 = lax.broadcasted_iota(jnp.int32, (24, 128), 1)
    first, last = lane == 0, lane == 127
    above = jnp.where(sub == 0, 0.0, 0.5)
    below = jnp.where(sub == 7, 0.0, 0.5)
    yes_left = jnp.where(left_in, 1.0, 0.0)
    yes_right = jnp.where(right_in, 1.0, 0.0)


    def fine_copies(n, array, h):
        ends = (
            (array.at[0, pl.ds(28 - h, h)], array.at[0, pl.ds(12 - h, h)]),
            (array.at[0, pl.ds(12, h)], array.at[0, pl.ds(28, h)]),
            (PS.at[n], PR.at[n, 0, pl.ds(3, 4)]),
            (PS.at[n], PR.at[n, 1, pl.ds(3, 4)]),
            (PS.at[n, pl.ds(2, 2)], PR.at[n, 0, pl.ds(1, 2)]),
            (PS.at[n, pl.ds(2, 2)], PR.at[n, 1, pl.ds(1, 2)]),
            (PS.at[n, pl.ds(0, 2)], PR.at[n, 0, pl.ds(7, 2)]),
            (PS.at[n, pl.ds(0, 2)], PR.at[n, 1, pl.ds(7, 2)]),
        )
        return [copy(a, b, FINE + 8 * n + i, at(*SIDES[i])) for i, (a, b) in enumerate(ends)]

    def more_copies(n, array, h):
        ends = (
            (array.at[0, pl.ds(24 - h, 4)], array.at[0, pl.ds(8 - h, 4)], 0),
            (array.at[0, pl.ds(12 + h, 4)], array.at[0, pl.ds(28 + h, 4)], 1),
            (PS.at[n, 1], PR.at[n, 0, 0], 4),
            (PS.at[n, 1], PR.at[n, 1, 0], 5),
            (PS.at[n, 2], PR.at[n, 0, 9], 6),
            (PS.at[n, 2], PR.at[n, 1, 9], 7),
        )
        return [copy(a, b, FINE_MORE + 6 * n + i, at(*SIDES[k])) for i, (a, b, k) in enumerate(ends)]

    def pack_edges(n, array):
        for b in range(4):
            packed = None
            for i in range(4):
                row = roll(array[0, OWN + 4 * b + i], 32 * i + 16, 1)
                packed = row if packed is None else jnp.where(lane >= 32 * i, row, packed)
            PS[n, b] = packed

    def unpack_edges(n, array, blocks, lo, hi):
        from_left = lax.rem(lane, 32) < 16
        for b in blocks:
            packed = jnp.where(from_left, PR[n, 0, b], PR[n, 1, b])
            for i in range(4):
                if lo <= 4 * b + i < hi:
                    array[1, 4 * b + i] = roll(packed, -(32 * i + 16), 1)

    def blur_row(t0, t1):
        b0, b1 = roll(t0, -1, 1), roll(t1, -1, 1)
        u0 = t0 + jnp.where(last, b1, b0)
        u1 = t1 + jnp.where(last, b0, b1)
        a0, a1 = roll(u0, 1, 1), roll(u1, 1, 1)
        y0 = u0 + jnp.where(first, a1, a0)
        y1 = u1 + jnp.where(first, a0, a1)
        return [y + (above * roll(y, 1, 0) + below * roll(y, -1, 0)) for y in (y0, y1)]

    def blur_rows(row, lo, hi, use, flux=True):
        before = pair = None
        for r in range(lo - 1, hi + 1):
            v = row(r)
            fields = [v, [C[t, r] * v[t] for t in range(2)]] if flux else [v]
            now = [blur_row(*f) for f in fields]
            if before is not None:
                two = [[a + b for a, b in zip(x, y)] for x, y in zip(before, now)]
                if pair is not None:
                    use(r - 1, *[[a + b for a, b in zip(x, y)] for x, y in zip(pair, two)])
                pair = two
            before = now

    def fine_change(q, t, v, f, spread, flux):
        return f[t, q] - (D[t, q] * v - (C[t, q] * spread[t] + flux[t]))

    def fine_sweep(source, row, lo, hi, keep):
        def use(q, spread, flux):
            v = row(q)
            for t in range(2):
                keep(t, q, v[t] + W[t, q] * fine_change(q, t, v[t], source, spread, flux))

        blur_rows(row, lo, hi, use)

    def rows_of(array):
        return lambda r: [array[0, r], array[1, r]]

    def put(array):
        def keep(t, q, v):
            array[t, q] = v

        return keep

    def mask_conductivity(rows):
        side = jnp.where(lane < 64, yes_right, yes_left)
        for r in rows:
            if OWN <= r < OWN + WIDE:
                C[1, r] = C[1, r] * side
            else:
                mask = low_in if r < OWN else high_in
                C[0, r] = C[0, r] * mask
                C[1, r] = C[1, r] * (side * mask)

    def coefficients(q, spread):
        for t in range(2):
            c = C[t, q]
            diag = (4.0 * (6.0 + SHIFT)) * c + spread[t]
            inside = c > 0.0
            D[t, q] = diag + 8.0 * c
            W[t, q] = jnp.where(inside, RELAX / jnp.where(inside, diag, 1.0), 0.0)

    def fine_pairs(t):
        return [T[t, pl.ds(2 * d, 24, stride=8), :] + T[t, pl.ds(2 * d + 1, 24, stride=8), :] for d in range(4)]

    twice = lax.rem(2 * lane24, 128)

    def along_pairs(v, index):
        return pick(v + roll(v, -1, 1), index)


    def two_in_one(a, b):
        return jnp.where(lane < 64, a, roll(b, 64, 1))

    def mid_copies(number, source, target):
        return [copy(source, target.at[i], number, at(*SIDES[i])) for i in range(8)]

    def mid_whole(own, arrived, keep):
        for g, (middle, before, after) in enumerate(((0, 4, 5), (None, 2, 3), (1, 6, 7))):
            for d in range(own.shape[0]):
                m = own[d] if middle is None else arrived[middle, d]
                outer = jnp.where(lane < 32, arrived[after, d], arrived[before, d])
                outer2 = jnp.where(lane < 96, arrived[after, d], arrived[before, d])
                keep(g, d, jnp.where(lane < 64, m, roll(outer, 64, 1)), jnp.where(lane < 64, roll(m, 64, 1), outer2))

    def stack_depth(a, b):
        return jnp.where(sub < 4, a, roll(b, 4, 0))


    spot = 2 * lax.rem(lane, 32)
    mid_side = jnp.where(lane < 64, 1.0, jnp.where(lane < 96, yes_right, yes_left))
    masks = (mid_side * low_in, mid_side, mid_side * high_in)

    def far_copies(n, target, peers):
        return [copy(AS.at[n], target.at[i], FAR + n, at(*p)) for i, p in enumerate(peers)]

    def far_block(n, arrived, peers, a, split):
        parts = []
        for b in (-1, 0, 1):
            parts.append(AS[n] if (a, b) == (0, 0) else arrived[peers.index((-a, -b))])
        if not split:
            return [jnp.where(lane < 32, parts[0], jnp.where(lane < 64, parts[1], parts[2]))]
        turned = [roll(p, 32, 1) for p in parts]
        return [
            jnp.where(lane < 32, parts[0], jnp.where(lane < 64, turned[1], parts[2])),
            jnp.where(lane < 32, turned[0], jnp.where(lane < 64, parts[1], turned[2])),
        ]

    def spread_far(n, arrived, peers, arrays, mask):
        split = len(arrays) == 2
        zero = jnp.zeros((8, 128), jnp.float32)
        reach = max(p[0] for p in peers)
        for g in range(6):
            pair = []
            for a in (2 * g - 5, 2 * g - 4):
                blocks = far_block(n, arrived, peers, a, split) if abs(a) <= reach else [zero] * len(arrays)
                if mask is not None and abs(a) <= reach:
                    there = jnp.where(jnp.logical_and(gx + a >= 0, gx + a < gx_count), 1.0, 0.0)
                    blocks[0] = blocks[0] * (mask * there)
                pair.append(blocks)
            for j, array in enumerate(arrays):
                array[0, 8 * g : 8 * g + 8, :] = stack_depth(pair[0][j], pair[1][j])
                array[1, 8 * g : 8 * g + 8, :] = jnp.where(sub < 4, roll(pair[0][j], 4, 0), pair[1][j])

    def load(ref, count):
        return [ref[d] for d in range(count)]

    ends = []

    def start(copies, group=None):
        for c in copies:
            c.start()
        if group is None:
            ends.extend(copies)
            return copies
        buffer, number = group
        whole = [copy(buffer, buffer, number, at(1, 0))]
        ends.extend(whole)
        return whole

    def arrive(copies):
        for c in copies:
            c.wait_recv()

    T[...] = jnp.zeros_like(T)
    G[...] = jnp.zeros_like(G)
    for c in inputs:
        c.wait()
    for x in range(WIDE):
        where = pl.ds(x, DEPTH, stride=WIDE)
        lost = 1.0 - look_up(charge[where, :], charge_table)
        C[0, OWN + x] = (look_up(cond[where, :], cond_table) * 0.25) * lost
        F[0, 0, OWN + x] = rhs[where, :]
    pack_edges(0, C)
    pack_edges(1, F.at[0])
    for q in range(8, 16):
        r = 2 * q - 4
        T[0, 8 * q : 8 * q + 8, :] = C[0, r] + C[0, r + 1]
    own = [along_pairs(v, twice)[8:16] * (0.125 * 0.125) for v in fine_pairs(0)]
    for d in range(2):
        E1[d] = two_in_one(own[d], own[d + 2])

    pl.semaphore_wait(barrier, len(AROUND))
    to_c = start(fine_copies(0, C, 7))
    to_f = start(fine_copies(1, F.at[0], 6))
    to_c1 = start(mid_copies(MID, E1, R1), (R1, MID))
    to_more = start(more_copies(0, C, 7)) + start(more_copies(1, F.at[0], 6))

    arrive(to_c)
    unpack_edges(0, C, range(1, 9), 5, 35)
    mask_conductivity(range(5, 35))
    blur_rows(rows_of(C), 6, 34, coefficients, flux=False)

    for cycle in range(CYCLES):
        source = F.at[cycle]
        final = cycle + 1 == CYCLES
        wide = 0 if final else 6

        if cycle == 0:
            arrive(to_f)
            unpack_edges(1, source, range(1, 9), 6, 34)

        def scaled(r):
            return [W[t, r] * source[t, r] for t in range(2)]

        fine_sweep(source, scaled, 7, 33, put(VB))
        held = {}

        def pair_up(q, spread, flux):
            v = [VB[0, q], VB[1, q]]
            for t in range(2):
                change = fine_change(q, t, v[t], source, spread, flux)
                if q % 2 == 0:
                    held[t] = change
                else:
                    at_row = 8 * (2 + q // 2)
                    T[t, at_row : at_row + 8, :] = held[t] + change

        blur_rows(rows_of(VB), 8, 32, pair_up)
        for d, (v0, v1) in enumerate(zip(fine_pairs(0), fine_pairs(1))):
            F1[d] = jnp.where(lane24 < 64, along_pairs(v0, twice), along_pairs(v1, twice)) * 0.125

        if cycle == 0:
            arrive(to_c1)

            def keep_c1(g, d, a, b):
                C1[d, 8 * g : 8 * g + 8, :] = a * masks[g]
                C1[d + 2, 8 * g : 8 * g + 8, :] = b * masks[g]

            mid_whole(E1, R1, keep_c1)
            c1 = load(C1, 4)
            diag = diagonal(c1, 1, 8.0)
            for d, w in enumerate(weight(c1, diag)):
                W1[d] = w
                D1[d] = diag[d] + 16.0 * c1[d]
            for d in range(2):
                G[d, 0:24, :] = c1[2 * d] + c1[2 * d + 1]
            c2 = []
            own = []
            for d in range(2):
                pairs = G[d, pl.ds(0, 16, stride=2), :] + G[d, pl.ds(1, 16, stride=2), :]
                c2.append(along_pairs(pairs, twice[:16]) * (0.125 * 0.25))
                pairs = G[d, pl.ds(8, 8, stride=2), :] + G[d, pl.ds(9, 8, stride=2), :]
                own.append(along_pairs(pairs, spot) * (0.125 * 0.25))
            own_d = []
            for d, v in enumerate(diagonal(c2, 2, 8.0)):
                S2[d] = v
                own_d.append(pick(S2[d, 4:12, :], spot // 2))
            AS[0] = jnp.where(lax.rem(lane, 64) < 32, stack_depth(*own), stack_depth(*own_d))
            to_far_c = start(far_copies(0, BC, AROUND), (BC, FAR))

        c1, w1, big1 = load(C1, 4), load(W1, 4), load(D1, 4)
        f1 = load(F1, 4)
        v1 = sweep([w * f for w, f in zip(w1, f1)], f1, c1, w1, big1)
        r1 = residual_of(v1, f1, c1, big1)
        own = []
        for d in range(2):
            G[d, 0:24, :] = r1[2 * d] + r1[2 * d + 1]
            pairs = G[d, pl.ds(8, 8, stride=2), :] + G[d, pl.ds(9, 8, stride=2), :]
            own.append(along_pairs(pairs, spot) * 0.125)
        AS[1 + cycle] = stack_depth(*own)
        peers, arrived = (NEARER, BL) if final else (AROUND, BF)
        to_far = start(far_copies(1 + cycle, arrived, peers), (arrived, FAR + 1 + cycle))
        for d in range(4):
            V1[d] = v1[d]
            E2[cycle, d] = two_in_one(F1[d, 8:16, :], V1[d, 8:16, :])
        to_mid = start(mid_copies(MID + 1 + cycle, E2.at[cycle], R2.at[cycle]), (R2.at[cycle], MID + 1 + cycle))

        if cycle == 0:
            arrive(to_more)
            unpack_edges(0, C, (0, 1, 8, 9), 1, 5)
            unpack_edges(0, C, (8, 9), 35, 39)
            unpack_edges(1, source, (0, 1), 2, 6)
            unpack_edges(1, source, (8, 9), 34, 38)
            mask_conductivity([*range(1, 5), *range(35, 39)])
            blur_rows(rows_of(C), 2, 6, coefficients, flux=False)
            blur_rows(rows_of(C), 34, 38, coefficients, flux=False)
            fine_sweep(source, scaled, 3, 7, put(VB))
            fine_sweep(source, scaled, 33, 37, put(VB))

            arrive(to_far_c)
            side = jnp.where(lane < 32, yes_left, jnp.where(lane < 64, 1.0, yes_right))
            spread_far(0, BC, AROUND, (C2, D2), side)
            c2 = load(C2, 2)
            diag = load(D2, 2)
            for d, w in enumerate(weight(c2, diag)):
                W2[d] = w
                D2[d] = diag[d] + 16.0 * c2[d]
            G3[...] = c2[0] + c2[1]
            pairs = G3[pl.ds(0, 24, stride=2), :] + G3[pl.ds(1, 24, stride=2), :]
            c3 = [along_pairs(pairs, twice) * (0.125 * 0.5)]
            diag = diagonal(c3, 3, 4.0)
            w3 = weight(c3, diag)
            big3 = [diag[0] + 8.0 * c3[0]]
            for j, v in enumerate((c3, w3, big3)):
                Z[j] = v[0]

        arrive(to_mid)

        def keep_1(g, d, a, b):
            F1[d, 8 * g : 8 * g + 8, :] = a
            V1[d, 8 * g : 8 * g + 8, :] = b * masks[g]

        mid_whole(E2.at[cycle], R2.at[cycle], keep_1)

        arrive(to_far)
        spread_far(1 + cycle, arrived, peers, (F2,), None)
        c2, w2, big2, f2 = load(C2, 2), load(W2, 2), load(D2, 2), load(F2, 2)
        v2 = sweep([w * f for w, f in zip(w2, f2)], f2, c2, w2, big2)
        for d in range(2):
            V2[d] = v2[d]
        r2 = residual_of(v2, f2, c2, big2)
        G3[...] = r2[0] + r2[1]

        pairs = G3[pl.ds(0, 24, stride=2), :] + G3[pl.ds(1, 24, stride=2), :]
        f3 = [along_pairs(pairs, twice) * 0.125]
        c3, w3, big3 = [Z[0]], [Z[1]], [Z[2]]
        v3 = [w3[0] * f3[0]]
        for _ in range(COARSE_SWEEPS - 1):
            v3 = sweep(v3, f3, c3, w3, big3)
        half = lane24 // 2
        up = pick(v3[0], half)
        H2[pl.ds(0, 24, stride=2), :] = up
        H2[pl.ds(1, 24, stride=2), :] = up

        c2, w2, big2, f2 = [[ref[d, 8:32, :] for d in range(2)] for ref in (C2, W2, D2, F2)]
        v2 = [V2[d, 8:32, :] + H2[8:32, :] for d in range(2)]
        for _ in range(2):
            v2 = sweep(v2, f2, c2, w2, big2)
        down = jnp.where(lane24 < 96, 32 + half, half - 32)
        for d in range(2):
            up = pick(v2[d], down)
            H1[d, pl.ds(0, 24, stride=2), :] = up
            H1[d, pl.ds(1, 24, stride=2), :] = up

        c1, w1, big1, f1 = load(C1, 4), load(W1, 4), load(D1, 4), load(F1, 4)
        v1 = [V1[d] + H1[d // 2, 16:40, :] for d in range(4)]
        for _ in range(2):
            v1 = sweep(v1, f1, c1, w1, big1)
        for d in range(8):
            T[0, pl.ds(d, 24, stride=8), :] = v1[d // 2]

        near = lane // 2
        for q in range((9 - wide) // 2 + 2, (30 + wide) // 2 + 3):
            row = T[0, 8 * q : 8 * q + 8, :]
            up = [pick(row, near), pick(row, 64 + near)]
            for r in (2 * q - 4, 2 * q - 3):
                for t in range(2):
                    VA[t, r] = VB[t, r] + up[t]
        fine_sweep(source, rows_of(VA), 10 - wide, 30 + wide, put(VB))

        def add(t, q, v):
            K[t, q] = v if cycle == 0 else K[t, q] + v

        fine_sweep(source, rows_of(VB), 11 - wide, 29 + wide, add)

        def keep_residual(q, spread, flux):
            if final:
                v = K[0, q]
                out[pl.ds(q - OWN, DEPTH, stride=WIDE), :] = v
                res[pl.ds(q - OWN, DEPTH, stride=WIDE), :] = fine_change(q, 0, v, F.at[0], spread, flux)
            else:
                for t in range(2):
                    F[cycle + 1, t, q] = fine_change(q, t, K[t, q], F.at[0], spread, flux)

        blur_rows(rows_of(K), 12 - wide, 28 + wide, keep_residual)

    for c in ends:
        c.wait_send()


def per_device(gx_count, gy_count, rhs, cond_class, charge_class, cond_table, charge_table):
    flat = (DEPTH * WIDE, LONG)
    f32, i32 = jnp.float32, jnp.int32
    tile = (8, 128)
    fine = pltpu.VMEM((2, 40) + tile, f32)
    mid = pltpu.VMEM((4, 24, 128), f32)
    low = pltpu.VMEM((2, 48, 128), f32)
    scratch = [
        pltpu.VMEM(flat, f32), pltpu.VMEM(flat, i32), pltpu.VMEM(flat, i32), pltpu.SMEM((16,), f32), pltpu.SMEM((16,), f32),
        fine, fine, fine, pltpu.VMEM((CYCLES, 2, 40) + tile, f32), fine, fine, fine,
        pltpu.VMEM((2, 4) + tile, f32), pltpu.VMEM((2, 2, 10) + tile, f32), pltpu.VMEM((2, 192, 128), f32),
        mid, mid, mid, mid, mid,
        pltpu.VMEM((2,) + tile, f32), pltpu.VMEM((8, 2) + tile, f32),
        pltpu.VMEM((CYCLES, 4) + tile, f32), pltpu.VMEM((CYCLES, 8, 4) + tile, f32),
        pltpu.VMEM((2, 32, 128), f32), pltpu.VMEM((2, 16, 128), f32),
        pltpu.VMEM((1 + CYCLES,) + tile, f32), pltpu.VMEM((len(AROUND),) + tile, f32),
        pltpu.VMEM((len(AROUND),) + tile, f32), pltpu.VMEM((len(NEARER),) + tile, f32),
        low, low, low, low, low, pltpu.VMEM((48, 128), f32),
        pltpu.VMEM((48, 128), f32), pltpu.VMEM((2, 48, 128), f32), pltpu.VMEM((3, 24, 128), f32),
        pltpu.SemaphoreType.DMA((COPIES,)), pltpu.SemaphoreType.DMA((COPIES,)), pltpu.SemaphoreType.DMA((5,)),
    ]
    hbm, vmem = pl.BlockSpec(memory_space=pl.ANY), pl.BlockSpec(memory_space=pltpu.VMEM)
    correction, residual = pl.pallas_call(
        functools.partial(kernel, gx_count, gy_count),
        out_shape=[pltpu.VMEM(flat, f32)] * 2,
        in_specs=[hbm] * 5,
        out_specs=[vmem, vmem],
        scratch_shapes=scratch,
        compiler_params=pltpu.CompilerParams(collective_id=0, has_side_effects=True),
    )(rhs.reshape(flat), cond_class.reshape(flat), charge_class.reshape(flat), cond_table, charge_table)
    return correction.reshape(rhs.shape), residual.reshape(rhs.shape)


def solution(mesh):
    placed = (P(None, "gx", "gy"), P(None, "gx", "gy"), P(None, "gx", "gy"), P(), P())
    return jax.shard_map(
        functools.partial(per_device, mesh.shape["gx"], mesh.shape["gy"]),
        mesh=mesh,
        in_specs=placed,
        out_specs=(P(None, "gx", "gy"), P(None, "gx", "gy")),
        check_vma=False,
    )
```

```python
import functools

import jax
import jax.numpy as jnp
from jax import lax
from jax.experimental import pallas as pl
from jax.experimental.pallas import tpu as pltpu
from jax.sharding import PartitionSpec as P

MESH = pl.DeviceIdType.MESH
CYCLES = 2
COARSE_SWEEPS = 6
RELAX = 0.9
SHIFT = 0.1
DEPTH, WIDE, LONG = 8, 16, 128
OWN = 12
SIDES = ((1, 0), (-1, 0), (0, 1), (0, -1), (1, 1), (1, -1), (-1, 1), (-1, -1))
AROUND = tuple((a, b) for a in range(-5, 6) for b in (-1, 0, 1) if (a, b) != (0, 0))
NEARER = tuple(p for p in AROUND if abs(p[0]) < 5)

FINE, FINE_MORE, MID, FAR = 0, 16, 28, 31
COPIES = 34


def roll(x, shift, axis):
    shift %= x.shape[axis]
    return pltpu.roll(x, shift, axis) if shift else x


def pick(x, index):
    return jnp.take_along_axis(x, index, axis=1)


def blur(fields):
    along = []
    for v in fields:
        y = (v + v) + (roll(v, 1, 1) + roll(v, -1, 1))
        along.append((y + y) + (roll(y, 1, 0) + roll(y, -1, 0)))
    if len(along) == 1:
        return along
    pairs = [along[0]] + [a + b for a, b in zip(along, along[1:])] + [along[-1]]
    return [a + b for a, b in zip(pairs, pairs[1:])]


def operate(v, c, big):
    spread = blur(v)
    flux = blur([a * b for a, b in zip(c, v)])
    return [g * a - (b * s + f) for g, a, b, s, f in zip(big, v, c, spread, flux)]


def sweep(v, f, c, w, big):
    return [a + q * (s - o) for a, q, s, o in zip(v, w, f, operate(v, c, big))]


def residual_of(v, f, c, big):
    return [s - o for s, o in zip(f, operate(v, c, big))]


def diagonal(c, level, scale):
    own = scale * (6.0 + SHIFT * 4.0**level)
    return [own * a + b for a, b in zip(c, blur(c))]


def weight(c, diag):
    return [jnp.where(a > 0.0, RELAX / jnp.where(a > 0.0, d, 1.0), 0.0) for a, d in zip(c, diag)]


def look_up(classes, table):
    bits = [(classes & (1 << b)) != 0 for b in range(4)]
    level = [table[i] for i in range(16)]
    for bit in bits:
        level = [jnp.where(bit, level[2 * i + 1], level[2 * i]) for i in range(len(level) // 2)]
    return level[0]


def kernel(gx_count, gy_count, rhs_in, cond_in, charge_in, cond_table_in, charge_table_in, out, res, *scratch):
    (rhs, cond, charge, cond_table, charge_table, C, W, D, F, VA, VB, K, PS, PR, T, C1, W1, D1, F1, V1, E1, R1, E2, R2, G, S2,
     AS, BC, BF, BL, C2, W2, D2, F2, V2, G3, H2, H1, Z, send_sem, recv_sem, in_sem) = scratch
    gx, gy = lax.axis_index("gx"), lax.axis_index("gy")

    def at(dx, dy):
        return (lax.rem(gx + (dx + gx_count), gx_count), lax.rem(gy + (dy + gy_count), gy_count))

    def copy(src, dst, number, where):
        return pltpu.make_async_remote_copy(
            src_ref=src, dst_ref=dst, send_sem=send_sem.at[number], recv_sem=recv_sem.at[number],
            device_id=where, device_id_type=MESH,
        )

    barrier = pltpu.get_barrier_semaphore()
    for peer in AROUND:
        pl.semaphore_signal(barrier, inc=1, device_id=at(*peer), device_id_type=MESH)
    pairs = ((cond_table_in, cond_table), (charge_table_in, charge_table), (cond_in, cond), (charge_in, charge), (rhs_in, rhs))
    inputs = [pltpu.make_async_copy(a, b, in_sem.at[i]) for i, (a, b) in enumerate(pairs)]
    for c in inputs:
        c.start()

    left_in, right_in = gy > 0, gy < gy_count - 1
    low_in = jnp.where(gx > 0, 1.0, 0.0)
    high_in = jnp.where(gx < gx_count - 1, 1.0, 0.0)
    lane = lax.broadcasted_iota(jnp.int32, (8, 128), 1)
    sub = lax.broadcasted_iota(jnp.int32, (8, 128), 0)
    lane24 = lax.broadcasted_iota(jnp.int32, (24, 128), 1)
    first, last = lane == 0, lane == 127
    above = jnp.where(sub == 0, 0.0, 0.5)
    below = jnp.where(sub == 7, 0.0, 0.5)
    yes_left = jnp.where(left_in, 1.0, 0.0)
    yes_right = jnp.where(right_in, 1.0, 0.0)


    def fine_copies(n, array, h):
        ends = (
            (array.at[0, pl.ds(28 - h, h)], array.at[0, pl.ds(12 - h, h)]),
            (array.at[0, pl.ds(12, h)], array.at[0, pl.ds(28, h)]),
            (PS.at[n], PR.at[n, 0, pl.ds(3, 4)]),
            (PS.at[n], PR.at[n, 1, pl.ds(3, 4)]),
            (PS.at[n, pl.ds(2, 2)], PR.at[n, 0, pl.ds(1, 2)]),
            (PS.at[n, pl.ds(2, 2)], PR.at[n, 1, pl.ds(1, 2)]),
            (PS.at[n, pl.ds(0, 2)], PR.at[n, 0, pl.ds(7, 2)]),
            (PS.at[n, pl.ds(0, 2)], PR.at[n, 1, pl.ds(7, 2)]),
        )
        return [copy(a, b, FINE + 8 * n + i, at(*SIDES[i])) for i, (a, b) in enumerate(ends)]

    def more_copies(n, array, h):
        ends = (
            (array.at[0, pl.ds(24 - h, 4)], array.at[0, pl.ds(8 - h, 4)], 0),
            (array.at[0, pl.ds(12 + h, 4)], array.at[0, pl.ds(28 + h, 4)], 1),
            (PS.at[n, 1], PR.at[n, 0, 0], 4),
            (PS.at[n, 1], PR.at[n, 1, 0], 5),
            (PS.at[n, 2], PR.at[n, 0, 9], 6),
            (PS.at[n, 2], PR.at[n, 1, 9], 7),
        )
        return [copy(a, b, FINE_MORE + 6 * n + i, at(*SIDES[k])) for i, (a, b, k) in enumerate(ends)]

    def pack_edges(n, array):
        for b in range(4):
            packed = None
            for i in range(4):
                row = roll(array[0, OWN + 4 * b + i], 32 * i + 16, 1)
                packed = row if packed is None else jnp.where(lane >= 32 * i, row, packed)
            PS[n, b] = packed

    def unpack_edges(n, array, blocks, lo, hi):
        from_left = lax.rem(lane, 32) < 16
        for b in blocks:
            packed = jnp.where(from_left, PR[n, 0, b], PR[n, 1, b])
            for i in range(4):
                if lo <= 4 * b + i < hi:
                    array[1, 4 * b + i] = roll(packed, -(32 * i + 16), 1)

    def blur_row(t0, t1):
        a0, a1, b0, b1 = roll(t0, 1, 1), roll(t1, 1, 1), roll(t0, -1, 1), roll(t1, -1, 1)
        y0 = (t0 + t0) + (jnp.where(first, a1, a0) + jnp.where(last, b1, b0))
        y1 = (t1 + t1) + (jnp.where(first, a0, a1) + jnp.where(last, b0, b1))
        return [y + (above * roll(y, 1, 0) + below * roll(y, -1, 0)) for y in (y0, y1)]

    def blur_rows(row, lo, hi, use, flux=True):
        before = pair = None
        for r in range(lo - 1, hi + 1):
            v = row(r)
            fields = [v, [C[t, r] * v[t] for t in range(2)]] if flux else [v]
            now = [blur_row(*f) for f in fields]
            if before is not None:
                two = [[a + b for a, b in zip(x, y)] for x, y in zip(before, now)]
                if pair is not None:
                    use(r - 1, *[[a + b for a, b in zip(x, y)] for x, y in zip(pair, two)])
                pair = two
            before = now

    def fine_change(q, t, v, f, spread, flux):
        return f[t, q] - (D[t, q] * v - (C[t, q] * spread[t] + flux[t]))

    def fine_sweep(source, row, lo, hi, keep):
        def use(q, spread, flux):
            v = row(q)
            for t in range(2):
                keep(t, q, v[t] + W[t, q] * fine_change(q, t, v[t], source, spread, flux))

        blur_rows(row, lo, hi, use)

    def rows_of(array):
        return lambda r: [array[0, r], array[1, r]]

    def put(array):
        def keep(t, q, v):
            array[t, q] = v

        return keep

    def mask_conductivity(rows):
        side = jnp.where(lane < 64, yes_right, yes_left)
        for r in rows:
            if OWN <= r < OWN + WIDE:
                C[1, r] = C[1, r] * side
            else:
                mask = low_in if r < OWN else high_in
                C[0, r] = C[0, r] * mask
                C[1, r] = C[1, r] * (side * mask)

    def coefficients(q, spread):
        for t in range(2):
            c = C[t, q]
            diag = (4.0 * (6.0 + SHIFT)) * c + spread[t]
            inside = c > 0.0
            D[t, q] = diag + 8.0 * c
            W[t, q] = jnp.where(inside, RELAX / jnp.where(inside, diag, 1.0), 0.0)

    def fine_pairs(t):
        return [T[t, pl.ds(2 * d, 24, stride=8), :] + T[t, pl.ds(2 * d + 1, 24, stride=8), :] for d in range(4)]

    twice = lax.rem(2 * lane24, 128)

    def along_pairs(v, index):
        return pick(v + roll(v, -1, 1), index)


    def two_in_one(a, b):
        return jnp.where(lane < 64, a, roll(b, 64, 1))

    def mid_copies(number, source, target):
        return [copy(source, target.at[i], number, at(*SIDES[i])) for i in range(8)]

    def mid_whole(own, arrived, keep):
        for g, (middle, before, after) in enumerate(((0, 4, 5), (None, 2, 3), (1, 6, 7))):
            for d in range(own.shape[0]):
                m = own[d] if middle is None else arrived[middle, d]
                outer = jnp.where(lane < 32, arrived[after, d], arrived[before, d])
                outer2 = jnp.where(lane < 96, arrived[after, d], arrived[before, d])
                keep(g, d, jnp.where(lane < 64, m, roll(outer, 64, 1)), jnp.where(lane < 64, roll(m, 64, 1), outer2))

    def stack_depth(a, b):
        return jnp.where(sub < 4, a, roll(b, 4, 0))


    spot = 2 * lax.rem(lane, 32)
    mid_side = jnp.where(lane < 64, 1.0, jnp.where(lane < 96, yes_right, yes_left))
    masks = (mid_side * low_in, mid_side, mid_side * high_in)

    def far_copies(n, target, peers):
        return [copy(AS.at[n], target.at[i], FAR + n, at(*p)) for i, p in enumerate(peers)]

    def far_block(n, arrived, peers, a, split):
        parts = []
        for b in (-1, 0, 1):
            parts.append(AS[n] if (a, b) == (0, 0) else arrived[peers.index((-a, -b))])
        if not split:
            return [jnp.where(lane < 32, parts[0], jnp.where(lane < 64, parts[1], parts[2]))]
        turned = [roll(p, 32, 1) for p in parts]
        return [
            jnp.where(lane < 32, parts[0], jnp.where(lane < 64, turned[1], parts[2])),
            jnp.where(lane < 32, turned[0], jnp.where(lane < 64, parts[1], turned[2])),
        ]

    def spread_far(n, arrived, peers, arrays, mask):
        split = len(arrays) == 2
        zero = jnp.zeros((8, 128), jnp.float32)
        reach = max(p[0] for p in peers)
        for g in range(6):
            pair = []
            for a in (2 * g - 5, 2 * g - 4):
                blocks = far_block(n, arrived, peers, a, split) if abs(a) <= reach else [zero] * len(arrays)
                if mask is not None and abs(a) <= reach:
                    there = jnp.where(jnp.logical_and(gx + a >= 0, gx + a < gx_count), 1.0, 0.0)
                    blocks[0] = blocks[0] * (mask * there)
                pair.append(blocks)
            for j, array in enumerate(arrays):
                array[0, 8 * g : 8 * g + 8, :] = stack_depth(pair[0][j], pair[1][j])
                array[1, 8 * g : 8 * g + 8, :] = jnp.where(sub < 4, roll(pair[0][j], 4, 0), pair[1][j])

    def load(ref, count):
        return [ref[d] for d in range(count)]

    ends = []

    def start(copies, group=None):
        for c in copies:
            c.start()
        if group is None:
            ends.extend(copies)
            return copies
        buffer, number = group
        whole = [copy(buffer, buffer, number, at(1, 0))]
        ends.extend(whole)
        return whole

    def arrive(copies):
        for c in copies:
            c.wait_recv()

    T[...] = jnp.zeros_like(T)
    G[...] = jnp.zeros_like(G)
    for c in inputs:
        c.wait()
    for x in range(WIDE):
        where = pl.ds(x, DEPTH, stride=WIDE)
        lost = 1.0 - look_up(charge[where, :], charge_table)
        C[0, OWN + x] = (look_up(cond[where, :], cond_table) * 0.25) * lost
        F[0, 0, OWN + x] = rhs[where, :]
    pack_edges(0, C)
    pack_edges(1, F.at[0])
    for q in range(8, 16):
        r = 2 * q - 4
        T[0, 8 * q : 8 * q + 8, :] = C[0, r] + C[0, r + 1]
    own = [along_pairs(v, twice)[8:16] * (0.125 * 0.125) for v in fine_pairs(0)]
    for d in range(2):
        E1[d] = two_in_one(own[d], own[d + 2])

    pl.semaphore_wait(barrier, len(AROUND))
    to_c = start(fine_copies(0, C, 7))
    to_f = start(fine_copies(1, F.at[0], 6))
    to_c1 = start(mid_copies(MID, E1, R1), (R1, MID))
    to_more = start(more_copies(0, C, 7)) + start(more_copies(1, F.at[0], 6))

    arrive(to_c)
    unpack_edges(0, C, range(1, 9), 5, 35)
    mask_conductivity(range(5, 35))
    blur_rows(rows_of(C), 6, 34, coefficients, flux=False)

    for cycle in range(CYCLES):
        source = F.at[cycle]
        final = cycle + 1 == CYCLES
        wide = 0 if final else 6

        if cycle == 0:
            arrive(to_f)
            unpack_edges(1, source, range(1, 9), 6, 34)

        def scaled(r):
            return [W[t, r] * source[t, r] for t in range(2)]

        fine_sweep(source, scaled, 7, 33, put(VB))
        held = {}

        def pair_up(q, spread, flux):
            v = [VB[0, q], VB[1, q]]
            for t in range(2):
                change = fine_change(q, t, v[t], source, spread, flux)
                if q % 2 == 0:
                    held[t] = change
                else:
                    at_row = 8 * (2 + q // 2)
                    T[t, at_row : at_row + 8, :] = held[t] + change

        blur_rows(rows_of(VB), 8, 32, pair_up)
        for d, (v0, v1) in enumerate(zip(fine_pairs(0), fine_pairs(1))):
            F1[d] = jnp.where(lane24 < 64, along_pairs(v0, twice), along_pairs(v1, twice)) * 0.125

        if cycle == 0:
            arrive(to_c1)

            def keep_c1(g, d, a, b):
                C1[d, 8 * g : 8 * g + 8, :] = a * masks[g]
                C1[d + 2, 8 * g : 8 * g + 8, :] = b * masks[g]

            mid_whole(E1, R1, keep_c1)
            c1 = load(C1, 4)
            diag = diagonal(c1, 1, 8.0)
            for d, w in enumerate(weight(c1, diag)):
                W1[d] = w
                D1[d] = diag[d] + 16.0 * c1[d]
            for d in range(2):
                G[d, 0:24, :] = c1[2 * d] + c1[2 * d + 1]
            c2 = []
            own = []
            for d in range(2):
                pairs = G[d, pl.ds(0, 16, stride=2), :] + G[d, pl.ds(1, 16, stride=2), :]
                c2.append(along_pairs(pairs, twice[:16]) * (0.125 * 0.25))
                pairs = G[d, pl.ds(8, 8, stride=2), :] + G[d, pl.ds(9, 8, stride=2), :]
                own.append(along_pairs(pairs, spot) * (0.125 * 0.25))
            own_d = []
            for d, v in enumerate(diagonal(c2, 2, 8.0)):
                S2[d] = v
                own_d.append(pick(S2[d, 4:12, :], spot // 2))
            AS[0] = jnp.where(lax.rem(lane, 64) < 32, stack_depth(*own), stack_depth(*own_d))
            to_far_c = start(far_copies(0, BC, AROUND), (BC, FAR))

        c1, w1, big1 = load(C1, 4), load(W1, 4), load(D1, 4)
        f1 = load(F1, 4)
        v1 = sweep([w * f for w, f in zip(w1, f1)], f1, c1, w1, big1)
        r1 = residual_of(v1, f1, c1, big1)
        own = []
        for d in range(2):
            G[d, 0:24, :] = r1[2 * d] + r1[2 * d + 1]
            pairs = G[d, pl.ds(8, 8, stride=2), :] + G[d, pl.ds(9, 8, stride=2), :]
            own.append(along_pairs(pairs, spot) * 0.125)
        AS[1 + cycle] = stack_depth(*own)
        peers, arrived = (NEARER, BL) if final else (AROUND, BF)
        to_far = start(far_copies(1 + cycle, arrived, peers), (arrived, FAR + 1 + cycle))
        for d in range(4):
            V1[d] = v1[d]
            E2[cycle, d] = two_in_one(F1[d, 8:16, :], V1[d, 8:16, :])
        to_mid = start(mid_copies(MID + 1 + cycle, E2.at[cycle], R2.at[cycle]), (R2.at[cycle], MID + 1 + cycle))

        if cycle == 0:
            arrive(to_more)
            unpack_edges(0, C, (0, 1, 8, 9), 1, 5)
            unpack_edges(0, C, (8, 9), 35, 39)
            unpack_edges(1, source, (0, 1), 2, 6)
            unpack_edges(1, source, (8, 9), 34, 38)
            mask_conductivity([*range(1, 5), *range(35, 39)])
            blur_rows(rows_of(C), 2, 6, coefficients, flux=False)
            blur_rows(rows_of(C), 34, 38, coefficients, flux=False)
            fine_sweep(source, scaled, 3, 7, put(VB))
            fine_sweep(source, scaled, 33, 37, put(VB))

            arrive(to_far_c)
            side = jnp.where(lane < 32, yes_left, jnp.where(lane < 64, 1.0, yes_right))
            spread_far(0, BC, AROUND, (C2, D2), side)
            c2 = load(C2, 2)
            diag = load(D2, 2)
            for d, w in enumerate(weight(c2, diag)):
                W2[d] = w
                D2[d] = diag[d] + 16.0 * c2[d]
            G3[...] = c2[0] + c2[1]
            pairs = G3[pl.ds(0, 24, stride=2), :] + G3[pl.ds(1, 24, stride=2), :]
            c3 = [along_pairs(pairs, twice) * (0.125 * 0.5)]
            diag = diagonal(c3, 3, 4.0)
            w3 = weight(c3, diag)
            big3 = [diag[0] + 8.0 * c3[0]]
            for j, v in enumerate((c3, w3, big3)):
                Z[j] = v[0]

        arrive(to_mid)

        def keep_1(g, d, a, b):
            F1[d, 8 * g : 8 * g + 8, :] = a
            V1[d, 8 * g : 8 * g + 8, :] = b * masks[g]

        mid_whole(E2.at[cycle], R2.at[cycle], keep_1)

        arrive(to_far)
        spread_far(1 + cycle, arrived, peers, (F2,), None)
        c2, w2, big2, f2 = load(C2, 2), load(W2, 2), load(D2, 2), load(F2, 2)
        v2 = sweep([w * f for w, f in zip(w2, f2)], f2, c2, w2, big2)
        for d in range(2):
            V2[d] = v2[d]
        r2 = residual_of(v2, f2, c2, big2)
        G3[...] = r2[0] + r2[1]

        pairs = G3[pl.ds(0, 24, stride=2), :] + G3[pl.ds(1, 24, stride=2), :]
        f3 = [along_pairs(pairs, twice) * 0.125]
        c3, w3, big3 = [Z[0]], [Z[1]], [Z[2]]
        v3 = [w3[0] * f3[0]]
        for _ in range(COARSE_SWEEPS - 1):
            v3 = sweep(v3, f3, c3, w3, big3)
        half = lane24 // 2
        up = pick(v3[0], half)
        H2[pl.ds(0, 24, stride=2), :] = up
        H2[pl.ds(1, 24, stride=2), :] = up

        c2, w2, big2, f2 = [[ref[d, 8:32, :] for d in range(2)] for ref in (C2, W2, D2, F2)]
        v2 = [V2[d, 8:32, :] + H2[8:32, :] for d in range(2)]
        for _ in range(2):
            v2 = sweep(v2, f2, c2, w2, big2)
        down = jnp.where(lane24 < 96, 32 + half, half - 32)
        for d in range(2):
            up = pick(v2[d], down)
            H1[d, pl.ds(0, 24, stride=2), :] = up
            H1[d, pl.ds(1, 24, stride=2), :] = up

        c1, w1, big1, f1 = load(C1, 4), load(W1, 4), load(D1, 4), load(F1, 4)
        v1 = [V1[d] + H1[d // 2, 16:40, :] for d in range(4)]
        for _ in range(2):
            v1 = sweep(v1, f1, c1, w1, big1)
        for d in range(8):
            T[0, pl.ds(d, 24, stride=8), :] = v1[d // 2]

        near = lane // 2
        for q in range((9 - wide) // 2 + 2, (30 + wide) // 2 + 3):
            row = T[0, 8 * q : 8 * q + 8, :]
            up = [pick(row, near), pick(row, 64 + near)]
            for r in (2 * q - 4, 2 * q - 3):
                for t in range(2):
                    VA[t, r] = VB[t, r] + up[t]
        fine_sweep(source, rows_of(VA), 10 - wide, 30 + wide, put(VB))

        def add(t, q, v):
            K[t, q] = v if cycle == 0 else K[t, q] + v

        fine_sweep(source, rows_of(VB), 11 - wide, 29 + wide, add)

        def keep_residual(q, spread, flux):
            if final:
                v = K[0, q]
                out[pl.ds(q - OWN, DEPTH, stride=WIDE), :] = v
                res[pl.ds(q - OWN, DEPTH, stride=WIDE), :] = fine_change(q, 0, v, F.at[0], spread, flux)
            else:
                for t in range(2):
                    F[cycle + 1, t, q] = fine_change(q, t, K[t, q], F.at[0], spread, flux)

        blur_rows(rows_of(K), 12 - wide, 28 + wide, keep_residual)

    for c in ends:
        c.wait_send()


def per_device(gx_count, gy_count, rhs, cond_class, charge_class, cond_table, charge_table):
    flat = (DEPTH * WIDE, LONG)
    f32, i32 = jnp.float32, jnp.int32
    tile = (8, 128)
    fine = pltpu.VMEM((2, 40) + tile, f32)
    mid = pltpu.VMEM((4, 24, 128), f32)
    low = pltpu.VMEM((2, 48, 128), f32)
    scratch = [
        pltpu.VMEM(flat, f32), pltpu.VMEM(flat, i32), pltpu.VMEM(flat, i32), pltpu.SMEM((16,), f32), pltpu.SMEM((16,), f32),
        fine, fine, fine, pltpu.VMEM((CYCLES, 2, 40) + tile, f32), fine, fine, fine,
        pltpu.VMEM((2, 4) + tile, f32), pltpu.VMEM((2, 2, 10) + tile, f32), pltpu.VMEM((2, 192, 128), f32),
        mid, mid, mid, mid, mid,
        pltpu.VMEM((2,) + tile, f32), pltpu.VMEM((8, 2) + tile, f32),
        pltpu.VMEM((CYCLES, 4) + tile, f32), pltpu.VMEM((CYCLES, 8, 4) + tile, f32),
        pltpu.VMEM((2, 32, 128), f32), pltpu.VMEM((2, 16, 128), f32),
        pltpu.VMEM((1 + CYCLES,) + tile, f32), pltpu.VMEM((len(AROUND),) + tile, f32),
        pltpu.VMEM((len(AROUND),) + tile, f32), pltpu.VMEM((len(NEARER),) + tile, f32),
        low, low, low, low, low, pltpu.VMEM((48, 128), f32),
        pltpu.VMEM((48, 128), f32), pltpu.VMEM((2, 48, 128), f32), pltpu.VMEM((3, 24, 128), f32),
        pltpu.SemaphoreType.DMA((COPIES,)), pltpu.SemaphoreType.DMA((COPIES,)), pltpu.SemaphoreType.DMA((5,)),
    ]
    hbm, vmem = pl.BlockSpec(memory_space=pl.ANY), pl.BlockSpec(memory_space=pltpu.VMEM)
    correction, residual = pl.pallas_call(
        functools.partial(kernel, gx_count, gy_count),
        out_shape=[pltpu.VMEM(flat, f32)] * 2,
        in_specs=[hbm] * 5,
        out_specs=[vmem, vmem],
        scratch_shapes=scratch,
        compiler_params=pltpu.CompilerParams(collective_id=0, has_side_effects=True),
    )(rhs.reshape(flat), cond_class.reshape(flat), charge_class.reshape(flat), cond_table, charge_table)
    return correction.reshape(rhs.shape), residual.reshape(rhs.shape)


def solution(mesh):
    placed = (P(None, "gx", "gy"), P(None, "gx", "gy"), P(None, "gx", "gy"), P(), P())
    return jax.shard_map(
        functools.partial(per_device, mesh.shape["gx"], mesh.shape["gy"]),
        mesh=mesh,
        in_specs=placed,
        out_specs=(P(None, "gx", "gy"), P(None, "gx", "gy")),
        check_vma=False,
    )
```

```python
import functools

import jax
import jax.numpy as jnp
from jax import lax
from jax.experimental import pallas as pl
from jax.experimental.pallas import tpu as pltpu
from jax.sharding import PartitionSpec as P

MESH = pl.DeviceIdType.MESH
CYCLES = 2
COARSE_SWEEPS = 6
RELAX = 0.9
SHIFT = 0.1
DEPTH, WIDE, LONG = 8, 16, 128
OWN = 12
SIDES = ((1, 0), (-1, 0), (0, 1), (0, -1), (1, 1), (1, -1), (-1, 1), (-1, -1))
AROUND = tuple((s * a, b) for b in (-1, 1, 0) for a in (5, 2, 3, 1, 4, 0) for s in ((1, -1) if a else (1,)) if a or b)
NEARER = tuple(p for p in AROUND if abs(p[0]) < 5)

FINE, FINE_MORE, MID, FAR = 0, 16, 28, 31
COPIES = 33


def roll(x, shift, axis):
    shift %= x.shape[axis]
    return pltpu.roll(x, shift, axis) if shift else x


def pick(x, index):
    return jnp.take_along_axis(x, index, axis=1)


def blur(fields):
    along = []
    for v in fields:
        y = (v + v) + (roll(v, 1, 1) + roll(v, -1, 1))
        along.append((y + y) + (roll(y, 1, 0) + roll(y, -1, 0)))
    if len(along) == 1:
        return along
    pairs = [along[0]] + [a + b for a, b in zip(along, along[1:])] + [along[-1]]
    return [a + b for a, b in zip(pairs, pairs[1:])]


def operate(v, c, big):
    spread = blur(v)
    flux = blur([a * b for a, b in zip(c, v)])
    return [g * a - (b * s + f) for g, a, b, s, f in zip(big, v, c, spread, flux)]


def sweep(v, f, c, w, big):
    return [a + q * (s - o) for a, q, s, o in zip(v, w, f, operate(v, c, big))]


def residual_of(v, f, c, big):
    return [s - o for s, o in zip(f, operate(v, c, big))]


def diagonal(c, level, scale):
    own = scale * (6.0 + SHIFT * 4.0**level)
    return [own * a + b for a, b in zip(c, blur(c))]


def weight(c, diag):
    return [jnp.where(a > 0.0, RELAX / jnp.where(a > 0.0, d, 1.0), 0.0) for a, d in zip(c, diag)]


def look_up(classes, table):
    bits = [(classes & (1 << b)) != 0 for b in range(4)]
    level = [table[i] for i in range(16)]
    for bit in bits:
        level = [jnp.where(bit, level[2 * i + 1], level[2 * i]) for i in range(len(level) // 2)]
    return level[0]


def kernel(gx_count, gy_count, rhs_in, cond_in, charge_in, cond_table_in, charge_table_in, out, res, *scratch):
    (rhs, cond, charge, cond_table, charge_table, C, W, D, F, VA, VB, K, PS, PR, T, C1, W1, D1, F1, V1, E1, R1, E2, R2, G, S2,
     AS, AL, BF, BL, C2, W2, D2, F2, V2, G3, H2, H1, Z, send_sem, recv_sem, in_sem) = scratch
    gx, gy = lax.axis_index("gx"), lax.axis_index("gy")

    def at(dx, dy):
        return (lax.rem(gx + (dx + gx_count), gx_count), lax.rem(gy + (dy + gy_count), gy_count))

    def copy(src, dst, number, where):
        return pltpu.make_async_remote_copy(
            src_ref=src, dst_ref=dst, send_sem=send_sem.at[number], recv_sem=recv_sem.at[number],
            device_id=where, device_id_type=MESH,
        )

    pairs = ((cond_table_in, cond_table), (charge_table_in, charge_table), (cond_in, cond), (charge_in, charge), (rhs_in, rhs))
    inputs = [pltpu.make_async_copy(a, b, in_sem.at[i]) for i, (a, b) in enumerate(pairs)]
    for c in inputs:
        c.start()
    barrier = pltpu.get_barrier_semaphore()
    for peer in AROUND:
        pl.semaphore_signal(barrier, inc=1, device_id=at(*peer), device_id_type=MESH)

    left_in, right_in = gy > 0, gy < gy_count - 1
    low_in = jnp.where(gx > 0, 1.0, 0.0)
    high_in = jnp.where(gx < gx_count - 1, 1.0, 0.0)
    lane = lax.broadcasted_iota(jnp.int32, (8, 128), 1)
    sub = lax.broadcasted_iota(jnp.int32, (8, 128), 0)
    lane24 = lax.broadcasted_iota(jnp.int32, (24, 128), 1)
    first, last = lane == 0, lane == 127
    above = jnp.where(sub == 0, 0.0, 0.5)
    below = jnp.where(sub == 7, 0.0, 0.5)
    yes_left = jnp.where(left_in, 1.0, 0.0)
    yes_right = jnp.where(right_in, 1.0, 0.0)


    def fine_copies(n, array, h):
        ends = (
            (array.at[0, pl.ds(28 - h, h)], array.at[0, pl.ds(12 - h, h)]),
            (array.at[0, pl.ds(12, h)], array.at[0, pl.ds(28, h)]),
            (PS.at[n], PR.at[n, 0, pl.ds(3, 4)]),
            (PS.at[n], PR.at[n, 1, pl.ds(3, 4)]),
            (PS.at[n, pl.ds(2, 2)], PR.at[n, 0, pl.ds(1, 2)]),
            (PS.at[n, pl.ds(2, 2)], PR.at[n, 1, pl.ds(1, 2)]),
            (PS.at[n, pl.ds(0, 2)], PR.at[n, 0, pl.ds(7, 2)]),
            (PS.at[n, pl.ds(0, 2)], PR.at[n, 1, pl.ds(7, 2)]),
        )
        return [copy(*ends[i], FINE + 8 * n + i, at(*SIDES[i])) for i in (4, 5, 6, 7, 0, 1, 2, 3)]

    def more_copies(n, array, h):
        ends = (
            (array.at[0, pl.ds(24 - h, 4)], array.at[0, pl.ds(8 - h, 4)], 0),
            (array.at[0, pl.ds(12 + h, 4)], array.at[0, pl.ds(28 + h, 4)], 1),
            (PS.at[n, 1], PR.at[n, 0, 0], 4),
            (PS.at[n, 1], PR.at[n, 1, 0], 5),
            (PS.at[n, 2], PR.at[n, 0, 9], 6),
            (PS.at[n, 2], PR.at[n, 1, 9], 7),
        )
        return [copy(a, b, FINE_MORE + 6 * n + i, at(*SIDES[k])) for i, (a, b, k) in enumerate(ends)]

    def pack_edges(n, array):
        for b in range(4):
            packed = None
            for i in range(4):
                row = roll(array[0, OWN + 4 * b + i], 32 * i + 16, 1)
                packed = row if packed is None else jnp.where(lane >= 32 * i, row, packed)
            PS[n, b] = packed

    def unpack_edges(n, array, blocks, lo, hi):
        from_left = lax.rem(lane, 32) < 16
        for b in blocks:
            packed = jnp.where(from_left, PR[n, 0, b], PR[n, 1, b])
            for i in range(4):
                if lo <= 4 * b + i < hi:
                    array[1, 4 * b + i] = roll(packed, -(32 * i + 16), 1)

    def blur_row(t0, t1):
        a0, a1, b0, b1 = roll(t0, 1, 1), roll(t1, 1, 1), roll(t0, -1, 1), roll(t1, -1, 1)
        y0 = (t0 + t0) + (jnp.where(first, a1, a0) + jnp.where(last, b1, b0))
        y1 = (t1 + t1) + (jnp.where(first, a0, a1) + jnp.where(last, b0, b1))
        return [y + (above * roll(y, 1, 0) + below * roll(y, -1, 0)) for y in (y0, y1)]

    def blur_rows(row, lo, hi, use, flux=True):
        before = pair = None
        for r in range(lo - 1, hi + 1):
            v = row(r)
            fields = [v, [C[t, r] * v[t] for t in range(2)]] if flux else [v]
            now = [blur_row(*f) for f in fields]
            if before is not None:
                two = [[a + b for a, b in zip(x, y)] for x, y in zip(before, now)]
                if pair is not None:
                    use(r - 1, *[[a + b for a, b in zip(x, y)] for x, y in zip(pair, two)])
                pair = two
            before = now

    def fine_change(q, t, v, f, spread, flux):
        return f[t, q] - (D[t, q] * v - (C[t, q] * spread[t] + flux[t]))

    def fine_sweep(source, row, lo, hi, keep):
        def use(q, spread, flux):
            v = row(q)
            for t in range(2):
                keep(t, q, v[t] + W[t, q] * fine_change(q, t, v[t], source, spread, flux))

        blur_rows(row, lo, hi, use)

    def rows_of(array):
        return lambda r: [array[0, r], array[1, r]]

    def put(array):
        def keep(t, q, v):
            array[t, q] = v

        return keep

    def mask_conductivity(rows):
        side = jnp.where(lane < 64, yes_right, yes_left)
        for r in rows:
            if OWN <= r < OWN + WIDE:
                C[1, r] = C[1, r] * side
            else:
                mask = low_in if r < OWN else high_in
                C[0, r] = C[0, r] * mask
                C[1, r] = C[1, r] * (side * mask)

    def coefficients(q, spread):
        for t in range(2):
            c = C[t, q]
            diag = (4.0 * (6.0 + SHIFT)) * c + spread[t]
            inside = c > 0.0
            D[t, q] = diag + 8.0 * c
            W[t, q] = jnp.where(inside, RELAX / jnp.where(inside, diag, 1.0), 0.0)

    def fine_pairs(t):
        return [T[t, pl.ds(2 * d, 24, stride=8), :] + T[t, pl.ds(2 * d + 1, 24, stride=8), :] for d in range(4)]

    twice = lax.rem(2 * lane24, 128)

    def along_pairs(v, index):
        return pick(v + roll(v, -1, 1), index)


    def two_in_one(a, b):
        return jnp.where(lane < 64, a, roll(b, 64, 1))

    def mid_copies(number, source, target):
        return [copy(source, target.at[i], number, at(*SIDES[i])) for i in range(8)]

    def mid_whole(own, arrived, keep):
        for g, (middle, before, after) in enumerate(((0, 4, 5), (None, 2, 3), (1, 6, 7))):
            for d in range(own.shape[0]):
                m = own[d] if middle is None else arrived[middle, d]
                outer = jnp.where(lane < 32, arrived[after, d], arrived[before, d])
                outer2 = jnp.where(lane < 96, arrived[after, d], arrived[before, d])
                keep(g, d, jnp.where(lane < 64, m, roll(outer, 64, 1)), jnp.where(lane < 64, roll(m, 64, 1), outer2))

    def stack_depth(a, b):
        return jnp.where(sub < 4, a, roll(b, 4, 0))


    spot = 2 * lax.rem(lane, 32)
    mid_side = jnp.where(lane < 64, 1.0, jnp.where(lane < 96, yes_right, yes_left))
    masks = (mid_side * low_in, mid_side, mid_side * high_in)

    def far_copies(n, source, target, peers):
        return [copy(source, target.at[i], FAR + n, at(*p)) for i, p in enumerate(peers)]

    def by_side(left, middle, right):
        return jnp.where(lane < 32, left, jnp.where(lane < 64, middle, right))

    def first_block(a):
        parts = [AS[0] if (a, b) == (0, 0) else BF[AROUND.index((-a, -b))] for b in (-1, 0, 1)]
        return [by_side(*[roll(v, 32 * (k - j), 1) for k, v in enumerate(parts)]) for j in range(3)]

    unfold = 32 * lax.rem(sub, 4) + lax.rem(lane, 32)

    def later_block(a):
        parts = []
        for b in (-1, 0, 1):
            if (a, b) == (0, 0):
                parts.append(AS[1])
            else:
                k = NEARER.index((-a, -b))
                rows = [jnp.broadcast_to(BL[k, d : d + 1, :], (8, 128)) for d in range(2)]
                parts.append(pick(jnp.where(sub < 4, *rows), unfold))
        return [by_side(*parts)]

    def spread_far(block, reach, arrays, mask):
        zero = jnp.zeros((8, 128), jnp.float32)
        for g in range(6):
            pair = []
            for a in (2 * g - 5, 2 * g - 4):
                blocks = block(a) if abs(a) <= reach else [zero] * len(arrays)
                if mask is not None and abs(a) <= reach:
                    there = jnp.where(jnp.logical_and(gx + a >= 0, gx + a < gx_count), 1.0, 0.0)
                    blocks[0] = blocks[0] * (mask * there)
                pair.append(blocks)
            for j, array in enumerate(arrays):
                array[0, 8 * g : 8 * g + 8, :] = stack_depth(pair[0][j], pair[1][j])
                array[1, 8 * g : 8 * g + 8, :] = jnp.where(sub < 4, roll(pair[0][j], 4, 0), pair[1][j])

    def load(ref, count):
        return [ref[d] for d in range(count)]

    ends = []

    def start(copies, group=None):
        for c in copies:
            c.start()
        if group is None:
            ends.extend(copies)
            return copies
        buffer, number = group
        whole = [copy(buffer, buffer, number, at(1, 0))]
        ends.extend(whole)
        return whole

    def arrive(copies):
        for c in copies:
            c.wait_recv()

    T[...] = jnp.zeros_like(T)
    G[...] = jnp.zeros_like(G)
    for c in inputs:
        c.wait()
    for x in range(WIDE):
        where = pl.ds(x, DEPTH, stride=WIDE)
        lost = 1.0 - look_up(charge[where, :], charge_table)
        C[0, OWN + x] = (look_up(cond[where, :], cond_table) * 0.25) * lost
        F[0, 0, OWN + x] = rhs[where, :]
    pack_edges(0, C)
    pack_edges(1, F.at[0])
    for q in range(8, 16):
        r = 2 * q - 4
        T[0, 8 * q : 8 * q + 8, :] = C[0, r] + C[0, r + 1]
    own = [along_pairs(v, twice)[8:16] * (0.125 * 0.125) for v in fine_pairs(0)]
    for d in range(2):
        E1[d] = two_in_one(own[d], own[d + 2])

    pl.semaphore_wait(barrier, len(AROUND))
    to_c = start(fine_copies(0, C, 7))
    to_f = start(fine_copies(1, F.at[0], 6))
    to_c1 = start(mid_copies(MID, E1, R1), (R1, MID))
    to_more = start(more_copies(0, C, 7)) + start(more_copies(1, F.at[0], 6))

    arrive(to_c)
    unpack_edges(0, C, range(1, 9), 5, 35)
    mask_conductivity(range(5, 35))
    blur_rows(rows_of(C), 6, 34, coefficients, flux=False)

    for cycle in range(CYCLES):
        source = F.at[cycle]
        final = cycle + 1 == CYCLES
        wide = 0 if final else 6

        if cycle == 0:
            arrive(to_f)
            unpack_edges(1, source, range(1, 9), 6, 34)

        def scaled(r):
            return [W[t, r] * source[t, r] for t in range(2)]

        fine_sweep(source, scaled, 7, 33, put(VB))
        held = {}

        def pair_up(q, spread, flux):
            v = [VB[0, q], VB[1, q]]
            for t in range(2):
                change = fine_change(q, t, v[t], source, spread, flux)
                if q % 2 == 0:
                    held[t] = change
                else:
                    at_row = 8 * (2 + q // 2)
                    T[t, at_row : at_row + 8, :] = held[t] + change

        blur_rows(rows_of(VB), 8, 32, pair_up)
        for d, (v0, v1) in enumerate(zip(fine_pairs(0), fine_pairs(1))):
            F1[d] = jnp.where(lane24 < 64, along_pairs(v0, twice), along_pairs(v1, twice)) * 0.125

        if cycle == 0:
            arrive(to_c1)

            def keep_c1(g, d, a, b):
                C1[d, 8 * g : 8 * g + 8, :] = a * masks[g]
                C1[d + 2, 8 * g : 8 * g + 8, :] = b * masks[g]

            mid_whole(E1, R1, keep_c1)
            c1 = load(C1, 4)
            diag = diagonal(c1, 1, 8.0)
            for d, w in enumerate(weight(c1, diag)):
                W1[d] = w
                D1[d] = diag[d] + 16.0 * c1[d]
            for d in range(2):
                G[d, 0:24, :] = c1[2 * d] + c1[2 * d + 1]
            c2 = []
            own_c = []
            for d in range(2):
                pairs = G[d, pl.ds(0, 16, stride=2), :] + G[d, pl.ds(1, 16, stride=2), :]
                c2.append(along_pairs(pairs, twice[:16]) * (0.125 * 0.25))
                pairs = G[d, pl.ds(8, 8, stride=2), :] + G[d, pl.ds(9, 8, stride=2), :]
                own_c.append(along_pairs(pairs, spot) * (0.125 * 0.25))
            own_d = []
            for d, v in enumerate(diagonal(c2, 2, 8.0)):
                S2[d] = v
                own_d.append(pick(S2[d, 4:12, :], spot // 2))

        c1, w1, big1 = load(C1, 4), load(W1, 4), load(D1, 4)
        f1 = load(F1, 4)
        v1 = sweep([w * f for w, f in zip(w1, f1)], f1, c1, w1, big1)
        r1 = residual_of(v1, f1, c1, big1)
        own = []
        for d in range(2):
            G[d, 0:24, :] = r1[2 * d] + r1[2 * d + 1]
            pairs = G[d, pl.ds(8, 8, stride=2), :] + G[d, pl.ds(9, 8, stride=2), :]
            own.append(along_pairs(pairs, spot) * 0.125)
        own = stack_depth(*own)
        if cycle == 0:
            AS[0] = jnp.where(lane < 32, stack_depth(*own_c), jnp.where(lane < 64, stack_depth(*own_d), own))
            to_far = start(far_copies(0, AS.at[0], BF, AROUND), (BF, FAR))
        else:
            AS[1] = own
            one = jnp.where(lane // 32 == lax.rem(sub, 4), own, 0.0)
            one = one + roll(one, -1, 0)
            one = one + roll(one, -2, 0)
            AL[...] = jnp.where(sub == 0, one, roll(one, -3, 0))[0:2]
            to_far = start(far_copies(1, AL, BL, NEARER), (BL, FAR + 1))
        for d in range(4):
            V1[d] = v1[d]
            E2[cycle, d] = two_in_one(F1[d, 8:16, :], V1[d, 8:16, :])
        to_mid = start(mid_copies(MID + 1 + cycle, E2.at[cycle], R2.at[cycle]), (R2.at[cycle], MID + 1 + cycle))

        if cycle == 0:
            arrive(to_more)
            unpack_edges(0, C, (0, 1, 8, 9), 1, 5)
            unpack_edges(0, C, (8, 9), 35, 39)
            unpack_edges(1, source, (0, 1), 2, 6)
            unpack_edges(1, source, (8, 9), 34, 38)
            mask_conductivity([*range(1, 5), *range(35, 39)])
            blur_rows(rows_of(C), 2, 6, coefficients, flux=False)
            blur_rows(rows_of(C), 34, 38, coefficients, flux=False)
            fine_sweep(source, scaled, 3, 7, put(VB))
            fine_sweep(source, scaled, 33, 37, put(VB))

        arrive(to_far)
        if cycle == 0:
            side = jnp.where(lane < 32, yes_left, jnp.where(lane < 64, 1.0, yes_right))
            spread_far(first_block, 5, (C2, D2, F2), side)
            c2 = load(C2, 2)
            diag = load(D2, 2)
            for d, w in enumerate(weight(c2, diag)):
                W2[d] = w
                D2[d] = diag[d] + 16.0 * c2[d]
        else:
            spread_far(later_block, 4, (F2,), None)
        c2, w2, big2, f2 = load(C2, 2), load(W2, 2), load(D2, 2), load(F2, 2)
        v2 = sweep([w * f for w, f in zip(w2, f2)], f2, c2, w2, big2)
        for d in range(2):
            V2[d] = v2[d]
        r2 = residual_of(v2, f2, c2, big2)
        if cycle == 0:
            G3[...] = c2[0] + c2[1]
            pairs = G3[pl.ds(0, 24, stride=2), :] + G3[pl.ds(1, 24, stride=2), :]
            c3 = [along_pairs(pairs, twice) * (0.125 * 0.5)]
            diag = diagonal(c3, 3, 4.0)
            w3 = weight(c3, diag)
            big3 = [diag[0] + 8.0 * c3[0]]
            for j, v in enumerate((c3, w3, big3)):
                Z[j] = v[0]
        H2[...] = r2[0] + r2[1]

        pairs = H2[pl.ds(0, 24, stride=2), :] + H2[pl.ds(1, 24, stride=2), :]
        f3 = [along_pairs(pairs, twice) * 0.125]
        c3, w3, big3 = [Z[0]], [Z[1]], [Z[2]]
        v3 = [w3[0] * f3[0]]
        for _ in range(COARSE_SWEEPS - 1):
            v3 = sweep(v3, f3, c3, w3, big3)
        half = lane24 // 2
        up = pick(v3[0], half)
        H2[pl.ds(0, 24, stride=2), :] = up
        H2[pl.ds(1, 24, stride=2), :] = up

        c2, w2, big2, f2 = [[ref[d, 8:32, :] for d in range(2)] for ref in (C2, W2, D2, F2)]
        v2 = [V2[d, 8:32, :] + H2[8:32, :] for d in range(2)]
        for _ in range(2):
            v2 = sweep(v2, f2, c2, w2, big2)
        down = jnp.where(lane24 < 96, 32 + half, half - 32)
        for d in range(2):
            up = pick(v2[d], down)
            H1[d, pl.ds(0, 24, stride=2), :] = up
            H1[d, pl.ds(1, 24, stride=2), :] = up

        arrive(to_mid)

        def keep_1(g, d, a, b):
            F1[d, 8 * g : 8 * g + 8, :] = a
            V1[d, 8 * g : 8 * g + 8, :] = b * masks[g]

        mid_whole(E2.at[cycle], R2.at[cycle], keep_1)
        c1, w1, big1, f1 = load(C1, 4), load(W1, 4), load(D1, 4), load(F1, 4)
        v1 = [V1[d] + H1[d // 2, 16:40, :] for d in range(4)]
        for _ in range(2):
            v1 = sweep(v1, f1, c1, w1, big1)
        for d in range(8):
            T[0, pl.ds(d, 24, stride=8), :] = v1[d // 2]

        near = lane // 2
        for q in range((9 - wide) // 2 + 2, (30 + wide) // 2 + 3):
            row = T[0, 8 * q : 8 * q + 8, :]
            up = [pick(row, near), pick(row, 64 + near)]
            for r in (2 * q - 4, 2 * q - 3):
                for t in range(2):
                    VA[t, r] = VB[t, r] + up[t]
        fine_sweep(source, rows_of(VA), 10 - wide, 30 + wide, put(VB))

        def add(t, q, v):
            K[t, q] = v if cycle == 0 else K[t, q] + v

        fine_sweep(source, rows_of(VB), 11 - wide, 29 + wide, add)

        def keep_residual(q, spread, flux):
            if final:
                v = K[0, q]
                out[pl.ds(q - OWN, DEPTH, stride=WIDE), :] = v
                res[pl.ds(q - OWN, DEPTH, stride=WIDE), :] = fine_change(q, 0, v, F.at[0], spread, flux)
            else:
                for t in range(2):
                    F[cycle + 1, t, q] = fine_change(q, t, K[t, q], F.at[0], spread, flux)

        blur_rows(rows_of(K), 12 - wide, 28 + wide, keep_residual)

    for c in ends:
        c.wait_send()


def per_device(gx_count, gy_count, rhs, cond_class, charge_class, cond_table, charge_table):
    flat = (DEPTH * WIDE, LONG)
    f32, i32 = jnp.float32, jnp.int32
    tile = (8, 128)
    fine = pltpu.VMEM((2, 40) + tile, f32)
    mid = pltpu.VMEM((4, 24, 128), f32)
    low = pltpu.VMEM((2, 48, 128), f32)
    scratch = [
        pltpu.VMEM(flat, f32), pltpu.VMEM(flat, i32), pltpu.VMEM(flat, i32), pltpu.SMEM((16,), f32), pltpu.SMEM((16,), f32),
        fine, fine, fine, pltpu.VMEM((CYCLES, 2, 40) + tile, f32), fine, fine, fine,
        pltpu.VMEM((2, 4) + tile, f32), pltpu.VMEM((2, 2, 10) + tile, f32), pltpu.VMEM((2, 192, 128), f32),
        mid, mid, mid, mid, mid,
        pltpu.VMEM((2,) + tile, f32), pltpu.VMEM((8, 2) + tile, f32),
        pltpu.VMEM((CYCLES, 4) + tile, f32), pltpu.VMEM((CYCLES, 8, 4) + tile, f32),
        pltpu.VMEM((2, 32, 128), f32), pltpu.VMEM((2, 16, 128), f32),
        pltpu.VMEM((2,) + tile, f32), pltpu.VMEM((2, 128), f32),
        pltpu.VMEM((len(AROUND),) + tile, f32), pltpu.VMEM((len(NEARER), 2, 128), f32),
        low, low, low, low, low, pltpu.VMEM((48, 128), f32),
        pltpu.VMEM((48, 128), f32), pltpu.VMEM((2, 48, 128), f32), pltpu.VMEM((3, 24, 128), f32),
        pltpu.SemaphoreType.DMA((COPIES,)), pltpu.SemaphoreType.DMA((COPIES,)), pltpu.SemaphoreType.DMA((5,)),
    ]
    hbm, vmem = pl.BlockSpec(memory_space=pl.ANY), pl.BlockSpec(memory_space=pltpu.VMEM)
    correction, residual = pl.pallas_call(
        functools.partial(kernel, gx_count, gy_count),
        out_shape=[pltpu.VMEM(flat, f32)] * 2,
        in_specs=[hbm] * 5,
        out_specs=[vmem, vmem],
        scratch_shapes=scratch,
        compiler_params=pltpu.CompilerParams(collective_id=0, has_side_effects=True),
    )(rhs.reshape(flat), cond_class.reshape(flat), charge_class.reshape(flat), cond_table, charge_table)
    return correction.reshape(rhs.shape), residual.reshape(rhs.shape)


def solution(mesh):
    placed = (P(None, "gx", "gy"), P(None, "gx", "gy"), P(None, "gx", "gy"), P(), P())
    return jax.shard_map(
        functools.partial(per_device, mesh.shape["gx"], mesh.shape["gy"]),
        mesh=mesh,
        in_specs=placed,
        out_specs=(P(None, "gx", "gy"), P(None, "gx", "gy")),
        check_vma=False,
    )
```

```python
import functools

import jax
import jax.numpy as jnp
from jax import lax
from jax.experimental import pallas as pl
from jax.experimental.pallas import tpu as pltpu
from jax.sharding import PartitionSpec as P

MESH = pl.DeviceIdType.MESH
CYCLES = 2
COARSE_SWEEPS = 6
RELAX = 0.9
SHIFT = 0.1
DEPTH, WIDE, LONG = 8, 16, 128
OWN = 12
SIDES = ((1, 0), (-1, 0), (0, 1), (0, -1), (1, 1), (1, -1), (-1, 1), (-1, -1))
AROUND = tuple((s * a, b) for b in (-1, 1, 0) for a in (5, 2, 3, 1, 4, 0) for s in ((1, -1) if a else (1,)) if a or b)
NEARER = tuple(p for p in AROUND if abs(p[0]) < 5)

FINE, FINE_MORE, MID, FAR = 0, 2, 4, 7
COPIES = 9


def roll(x, shift, axis):
    shift %= x.shape[axis]
    return pltpu.roll(x, shift, axis) if shift else x


def pick(x, index):
    return jnp.take_along_axis(x, index, axis=1)


def blur(fields):
    along = []
    for v in fields:
        y = (v + v) + (roll(v, 1, 1) + roll(v, -1, 1))
        along.append((y + y) + (roll(y, 1, 0) + roll(y, -1, 0)))
    if len(along) == 1:
        return along
    pairs = [along[0]] + [a + b for a, b in zip(along, along[1:])] + [along[-1]]
    return [a + b for a, b in zip(pairs, pairs[1:])]


def operate(v, c, big):
    spread = blur(v)
    flux = blur([a * b for a, b in zip(c, v)])
    return [g * a - (b * s + f) for g, a, b, s, f in zip(big, v, c, spread, flux)]


def sweep(v, f, c, w, big):
    return [a + q * (s - o) for a, q, s, o in zip(v, w, f, operate(v, c, big))]


def residual_of(v, f, c, big):
    return [s - o for s, o in zip(f, operate(v, c, big))]


def diagonal(c, level, scale):
    own = scale * (6.0 + SHIFT * 4.0**level)
    return [own * a + b for a, b in zip(c, blur(c))]


def weight(c, diag):
    return [jnp.where(a > 0.0, RELAX / jnp.where(a > 0.0, d, 1.0), 0.0) for a, d in zip(c, diag)]


def look_up(classes, table):
    bits = [(classes & (1 << b)) != 0 for b in range(4)]
    level = [table[i] for i in range(16)]
    for bit in bits:
        level = [jnp.where(bit, level[2 * i + 1], level[2 * i]) for i in range(len(level) // 2)]
    return level[0]


def kernel(gx_count, gy_count, rhs_in, cond_in, charge_in, cond_table_in, charge_table_in, out, res, *scratch):
    (rhs, cond, charge, cond_table, charge_table, C, W, D, F, VA, VB, K, PS, PR, T, C1, W1, D1, F1, V1, E1, R1, E2, R2, G, S2,
     AS, AL, BF, BL, C2, W2, D2, F2, V2, G3, H2, H1, Z, send_sem, recv_sem, in_sem) = scratch
    gx, gy = lax.axis_index("gx"), lax.axis_index("gy")

    def at(dx, dy):
        return (lax.rem(gx + (dx + gx_count), gx_count), lax.rem(gy + (dy + gy_count), gy_count))

    def copy(src, dst, number, where):
        return pltpu.make_async_remote_copy(
            src_ref=src, dst_ref=dst, send_sem=send_sem.at[number], recv_sem=recv_sem.at[number],
            device_id=where, device_id_type=MESH,
        )

    pairs = ((cond_table_in, cond_table), (charge_table_in, charge_table), (cond_in, cond), (charge_in, charge), (rhs_in, rhs))
    inputs = [pltpu.make_async_copy(a, b, in_sem.at[i]) for i, (a, b) in enumerate(pairs)]
    for c in inputs:
        c.start()
    barrier = pltpu.get_barrier_semaphore()
    for peer in AROUND:
        pl.semaphore_signal(barrier, inc=1, device_id=at(*peer), device_id_type=MESH)

    left_in, right_in = gy > 0, gy < gy_count - 1
    low_in = jnp.where(gx > 0, 1.0, 0.0)
    high_in = jnp.where(gx < gx_count - 1, 1.0, 0.0)
    lane = lax.broadcasted_iota(jnp.int32, (8, 128), 1)
    sub = lax.broadcasted_iota(jnp.int32, (8, 128), 0)
    lane24 = lax.broadcasted_iota(jnp.int32, (24, 128), 1)
    first, last = lane == 0, lane == 127
    above = jnp.where(sub == 0, 0.0, 0.5)
    below = jnp.where(sub == 7, 0.0, 0.5)
    yes_left = jnp.where(left_in, 1.0, 0.0)
    yes_right = jnp.where(right_in, 1.0, 0.0)


    def fine_copies(n, array, h):
        ends = (
            (array.at[0, pl.ds(28 - h, h)], array.at[0, pl.ds(12 - h, h)]),
            (array.at[0, pl.ds(12, h)], array.at[0, pl.ds(28, h)]),
            (PS.at[n], PR.at[n, 0, pl.ds(3, 4)]),
            (PS.at[n], PR.at[n, 1, pl.ds(3, 4)]),
            (PS.at[n, pl.ds(2, 2)], PR.at[n, 0, pl.ds(1, 2)]),
            (PS.at[n, pl.ds(2, 2)], PR.at[n, 1, pl.ds(1, 2)]),
            (PS.at[n, pl.ds(0, 2)], PR.at[n, 0, pl.ds(7, 2)]),
            (PS.at[n, pl.ds(0, 2)], PR.at[n, 1, pl.ds(7, 2)]),
        )
        return [copy(*ends[i], FINE + n, at(*SIDES[i])) for i in (4, 5, 6, 7, 0, 1, 2, 3)]

    def more_copies(n, array, h):
        ends = (
            (array.at[0, pl.ds(24 - h, 4)], array.at[0, pl.ds(8 - h, 4)], 0),
            (array.at[0, pl.ds(12 + h, 4)], array.at[0, pl.ds(28 + h, 4)], 1),
            (PS.at[n, 1], PR.at[n, 0, 0], 4),
            (PS.at[n, 1], PR.at[n, 1, 0], 5),
            (PS.at[n, 2], PR.at[n, 0, 9], 6),
            (PS.at[n, 2], PR.at[n, 1, 9], 7),
        )
        return [copy(a, b, FINE_MORE + n, at(*SIDES[k])) for i, (a, b, k) in enumerate(ends)]

    def pack_edges(n, array):
        for b in range(4):
            packed = None
            for i in range(4):
                row = roll(array[0, OWN + 4 * b + i], 32 * i + 16, 1)
                packed = row if packed is None else jnp.where(lane >= 32 * i, row, packed)
            PS[n, b] = packed

    def unpack_edges(n, array, blocks, lo, hi):
        from_left = lax.rem(lane, 32) < 16
        for b in blocks:
            packed = jnp.where(from_left, PR[n, 0, b], PR[n, 1, b])
            for i in range(4):
                if lo <= 4 * b + i < hi:
                    array[1, 4 * b + i] = roll(packed, -(32 * i + 16), 1)

    def blur_row(t0, t1):
        a0, a1, b0, b1 = roll(t0, 1, 1), roll(t1, 1, 1), roll(t0, -1, 1), roll(t1, -1, 1)
        y0 = (t0 + t0) + (jnp.where(first, a1, a0) + jnp.where(last, b1, b0))
        y1 = (t1 + t1) + (jnp.where(first, a0, a1) + jnp.where(last, b0, b1))
        return [y + (above * roll(y, 1, 0) + below * roll(y, -1, 0)) for y in (y0, y1)]

    def blur_rows(row, lo, hi, use, flux=True):
        before = pair = None
        for r in range(lo - 1, hi + 1):
            v = row(r)
            fields = [v, [C[t, r] * v[t] for t in range(2)]] if flux else [v]
            now = [blur_row(*f) for f in fields]
            if before is not None:
                two = [[a + b for a, b in zip(x, y)] for x, y in zip(before, now)]
                if pair is not None:
                    use(r - 1, *[[a + b for a, b in zip(x, y)] for x, y in zip(pair, two)])
                pair = two
            before = now

    def fine_change(q, t, v, f, spread, flux):
        return f[t, q] - (D[t, q] * v - (C[t, q] * spread[t] + flux[t]))

    def fine_sweep(source, row, lo, hi, keep):
        def use(q, spread, flux):
            v = row(q)
            for t in range(2):
                keep(t, q, v[t] + W[t, q] * fine_change(q, t, v[t], source, spread, flux))

        blur_rows(row, lo, hi, use)

    def rows_of(array):
        return lambda r: [array[0, r], array[1, r]]

    def put(array):
        def keep(t, q, v):
            array[t, q] = v

        return keep

    def mask_conductivity(rows):
        side = jnp.where(lane < 64, yes_right, yes_left)
        for r in rows:
            if OWN <= r < OWN + WIDE:
                C[1, r] = C[1, r] * side
            else:
                mask = low_in if r < OWN else high_in
                C[0, r] = C[0, r] * mask
                C[1, r] = C[1, r] * (side * mask)

    def coefficients(q, spread):
        for t in range(2):
            c = C[t, q]
            diag = (4.0 * (6.0 + SHIFT)) * c + spread[t]
            inside = c > 0.0
            D[t, q] = diag + 8.0 * c
            W[t, q] = jnp.where(inside, RELAX / jnp.where(inside, diag, 1.0), 0.0)

    def fine_pairs(t):
        return [T[t, pl.ds(2 * d, 24, stride=8), :] + T[t, pl.ds(2 * d + 1, 24, stride=8), :] for d in range(4)]

    twice = lax.rem(2 * lane24, 128)

    def along_pairs(v, index):
        return pick(v + roll(v, -1, 1), index)


    def two_in_one(a, b):
        return jnp.where(lane < 64, a, roll(b, 64, 1))

    def mid_copies(number, source, target):
        return [copy(source, target.at[i], number, at(*SIDES[i])) for i in (4, 5, 6, 7, 0, 1, 2, 3)]

    def mid_whole(own, arrived, keep):
        for g, (middle, before, after) in enumerate(((0, 4, 5), (None, 2, 3), (1, 6, 7))):
            for d in range(own.shape[0]):
                m = own[d] if middle is None else arrived[middle, d]
                outer = jnp.where(lane < 32, arrived[after, d], arrived[before, d])
                outer2 = jnp.where(lane < 96, arrived[after, d], arrived[before, d])
                keep(g, d, jnp.where(lane < 64, m, roll(outer, 64, 1)), jnp.where(lane < 64, roll(m, 64, 1), outer2))

    def stack_depth(a, b):
        return jnp.where(sub < 4, a, roll(b, 4, 0))


    spot = 2 * lax.rem(lane, 32)
    mid_side = jnp.where(lane < 64, 1.0, jnp.where(lane < 96, yes_right, yes_left))
    masks = (mid_side * low_in, mid_side, mid_side * high_in)

    def far_copies(n, source, target, peers):
        return [copy(source, target.at[i], FAR + n, at(*p)) for i, p in enumerate(peers)]

    def by_side(left, middle, right):
        return jnp.where(lane < 32, left, jnp.where(lane < 64, middle, right))

    def first_block(a):
        parts = [AS[0] if (a, b) == (0, 0) else BF[AROUND.index((-a, -b))] for b in (-1, 0, 1)]
        return [by_side(*[roll(v, 32 * (k - j), 1) for k, v in enumerate(parts)]) for j in range(3)]

    unfold = 32 * lax.rem(sub, 4) + lax.rem(lane, 32)

    def later_block(a):
        parts = []
        for b in (-1, 0, 1):
            if (a, b) == (0, 0):
                parts.append(AS[1])
            else:
                k = NEARER.index((-a, -b))
                rows = [jnp.broadcast_to(BL[k, d : d + 1, :], (8, 128)) for d in range(2)]
                parts.append(pick(jnp.where(sub < 4, *rows), unfold))
        return [by_side(*parts)]

    def spread_far(block, reach, arrays, mask):
        zero = jnp.zeros((8, 128), jnp.float32)
        for g in range(6):
            pair = []
            for a in (2 * g - 5, 2 * g - 4):
                blocks = block(a) if abs(a) <= reach else [zero] * len(arrays)
                if mask is not None and abs(a) <= reach:
                    there = jnp.where(jnp.logical_and(gx + a >= 0, gx + a < gx_count), 1.0, 0.0)
                    blocks[0] = blocks[0] * (mask * there)
                pair.append(blocks)
            for j, array in enumerate(arrays):
                array[0, 8 * g : 8 * g + 8, :] = stack_depth(pair[0][j], pair[1][j])
                array[1, 8 * g : 8 * g + 8, :] = jnp.where(sub < 4, roll(pair[0][j], 4, 0), pair[1][j])

    def load(ref, count):
        return [ref[d] for d in range(count)]

    ends = []

    def start(copies, group=None):
        for c in copies:
            c.start()
        if group is None:
            ends.extend(copies)
            return copies
        buffer, number = group
        whole = [copy(buffer, buffer, number, at(1, 0))]
        ends.extend(whole)
        return whole

    def arrive(copies):
        for c in copies:
            c.wait_recv()

    T[...] = jnp.zeros_like(T)
    G[...] = jnp.zeros_like(G)
    for c in inputs:
        c.wait()
    for x in range(WIDE):
        where = pl.ds(x, DEPTH, stride=WIDE)
        lost = 1.0 - look_up(charge[where, :], charge_table)
        C[0, OWN + x] = (look_up(cond[where, :], cond_table) * 0.25) * lost
        F[0, 0, OWN + x] = rhs[where, :]
    pack_edges(0, C)
    pack_edges(1, F.at[0])
    for q in range(8, 16):
        r = 2 * q - 4
        T[0, 8 * q : 8 * q + 8, :] = C[0, r] + C[0, r + 1]
    own = [along_pairs(v, twice)[8:16] * (0.125 * 0.125) for v in fine_pairs(0)]
    for d in range(2):
        E1[d] = two_in_one(own[d], own[d + 2])

    pl.semaphore_wait(barrier, len(AROUND))
    to_c = start(fine_copies(0, C, 7), (C.at[0, pl.ds(0, 30)], FINE))
    to_f = start(fine_copies(1, F.at[0], 6), (F.at[0, 0, pl.ds(0, 28)], FINE + 1))
    to_c1 = start(mid_copies(MID, E1, R1), (R1, MID))
    to_more = start(more_copies(0, C, 7), (C.at[0, pl.ds(0, 12)], FINE_MORE))
    to_more += start(more_copies(1, F.at[0], 6), (F.at[0, 0, pl.ds(0, 12)], FINE_MORE + 1))

    arrive(to_c)
    unpack_edges(0, C, range(1, 9), 5, 35)
    mask_conductivity(range(5, 35))
    blur_rows(rows_of(C), 6, 34, coefficients, flux=False)

    for cycle in range(CYCLES):
        source = F.at[cycle]
        final = cycle + 1 == CYCLES
        wide = 0 if final else 6

        if cycle == 0:
            arrive(to_f)
            unpack_edges(1, source, range(1, 9), 6, 34)

        def scaled(r):
            return [W[t, r] * source[t, r] for t in range(2)]

        fine_sweep(source, scaled, 7, 33, put(VB))
        held = {}

        def pair_up(q, spread, flux):
            v = [VB[0, q], VB[1, q]]
            for t in range(2):
                change = fine_change(q, t, v[t], source, spread, flux)
                if q % 2 == 0:
                    held[t] = change
                else:
                    at_row = 8 * (2 + q // 2)
                    T[t, at_row : at_row + 8, :] = held[t] + change

        blur_rows(rows_of(VB), 8, 32, pair_up)
        for d, (v0, v1) in enumerate(zip(fine_pairs(0), fine_pairs(1))):
            F1[d] = jnp.where(lane24 < 64, along_pairs(v0, twice), along_pairs(v1, twice)) * 0.125

        if cycle == 0:
            arrive(to_c1)

            def keep_c1(g, d, a, b):
                C1[d, 8 * g : 8 * g + 8, :] = a * masks[g]
                C1[d + 2, 8 * g : 8 * g + 8, :] = b * masks[g]

            mid_whole(E1, R1, keep_c1)
            c1 = load(C1, 4)
            diag = diagonal(c1, 1, 8.0)
            for d, w in enumerate(weight(c1, diag)):
                W1[d] = w
                D1[d] = diag[d] + 16.0 * c1[d]
            for d in range(2):
                G[d, 0:24, :] = c1[2 * d] + c1[2 * d + 1]
            c2 = []
            own_c = []
            for d in range(2):
                pairs = G[d, pl.ds(0, 16, stride=2), :] + G[d, pl.ds(1, 16, stride=2), :]
                c2.append(along_pairs(pairs, twice[:16]) * (0.125 * 0.25))
                pairs = G[d, pl.ds(8, 8, stride=2), :] + G[d, pl.ds(9, 8, stride=2), :]
                own_c.append(along_pairs(pairs, spot) * (0.125 * 0.25))
            own_d = []
            for d, v in enumerate(diagonal(c2, 2, 8.0)):
                S2[d] = v
                own_d.append(pick(S2[d, 4:12, :], spot // 2))

        c1, w1, big1 = load(C1, 4), load(W1, 4), load(D1, 4)
        f1 = load(F1, 4)
        v1 = sweep([w * f for w, f in zip(w1, f1)], f1, c1, w1, big1)
        r1 = residual_of(v1, f1, c1, big1)
        own = []
        for d in range(2):
            G[d, 0:24, :] = r1[2 * d] + r1[2 * d + 1]
            pairs = G[d, pl.ds(8, 8, stride=2), :] + G[d, pl.ds(9, 8, stride=2), :]
            own.append(along_pairs(pairs, spot) * 0.125)
        own = stack_depth(*own)
        if cycle == 0:
            AS[0] = jnp.where(lane < 32, stack_depth(*own_c), jnp.where(lane < 64, stack_depth(*own_d), own))
            to_far = start(far_copies(0, AS.at[0], BF, AROUND), (BF, FAR))
        else:
            AS[1] = own
            one = jnp.where(lane // 32 == lax.rem(sub, 4), own, 0.0)
            one = one + roll(one, -1, 0)
            one = one + roll(one, -2, 0)
            AL[...] = jnp.where(sub == 0, one, roll(one, -3, 0))[0:2]
            to_far = start(far_copies(1, AL, BL, NEARER), (BL, FAR + 1))

        def send_mid():
            return start(mid_copies(MID + 1 + cycle, E2.at[cycle], R2.at[cycle]), (R2.at[cycle], MID + 1 + cycle))

        for d in range(4):
            V1[d] = v1[d]
            E2[cycle, d] = two_in_one(F1[d, 8:16, :], V1[d, 8:16, :])
        to_mid = send_mid()

        if cycle == 0:
            arrive(to_more)
            unpack_edges(0, C, (0, 1, 8, 9), 1, 5)
            unpack_edges(0, C, (8, 9), 35, 39)
            unpack_edges(1, source, (0, 1), 2, 6)
            unpack_edges(1, source, (8, 9), 34, 38)
            mask_conductivity([*range(1, 5), *range(35, 39)])
            blur_rows(rows_of(C), 2, 6, coefficients, flux=False)
            blur_rows(rows_of(C), 34, 38, coefficients, flux=False)
            fine_sweep(source, scaled, 3, 7, put(VB))
            fine_sweep(source, scaled, 33, 37, put(VB))

        arrive(to_far)
        if cycle == 0:
            side = jnp.where(lane < 32, yes_left, jnp.where(lane < 64, 1.0, yes_right))
            spread_far(first_block, 5, (C2, D2, F2), side)
            c2 = load(C2, 2)
            diag = load(D2, 2)
            for d, w in enumerate(weight(c2, diag)):
                W2[d] = w
                D2[d] = diag[d] + 16.0 * c2[d]
        else:
            spread_far(later_block, 4, (F2,), None)
        c2, w2, big2, f2 = load(C2, 2), load(W2, 2), load(D2, 2), load(F2, 2)
        v2 = sweep([w * f for w, f in zip(w2, f2)], f2, c2, w2, big2)
        for d in range(2):
            V2[d] = v2[d]
        r2 = residual_of(v2, f2, c2, big2)
        if cycle == 0:
            G3[...] = c2[0] + c2[1]
            pairs = G3[pl.ds(0, 24, stride=2), :] + G3[pl.ds(1, 24, stride=2), :]
            c3 = [along_pairs(pairs, twice) * (0.125 * 0.5)]
            diag = diagonal(c3, 3, 4.0)
            w3 = weight(c3, diag)
            big3 = [diag[0] + 8.0 * c3[0]]
            for j, v in enumerate((c3, w3, big3)):
                Z[j] = v[0]
        H2[...] = r2[0] + r2[1]

        pairs = H2[pl.ds(0, 24, stride=2), :] + H2[pl.ds(1, 24, stride=2), :]
        f3 = [along_pairs(pairs, twice) * 0.125]
        c3, w3, big3 = [Z[0]], [Z[1]], [Z[2]]
        v3 = [w3[0] * f3[0]]
        for _ in range(COARSE_SWEEPS - 1):
            v3 = sweep(v3, f3, c3, w3, big3)
        half = lane24 // 2
        up = pick(v3[0], half)
        H2[pl.ds(0, 24, stride=2), :] = up
        H2[pl.ds(1, 24, stride=2), :] = up

        c2, w2, big2, f2 = [[ref[d, 8:32, :] for d in range(2)] for ref in (C2, W2, D2, F2)]
        v2 = [V2[d, 8:32, :] + H2[8:32, :] for d in range(2)]
        for _ in range(2):
            v2 = sweep(v2, f2, c2, w2, big2)
        down = jnp.where(lane24 < 96, 32 + half, half - 32)
        for d in range(2):
            up = pick(v2[d], down)
            H1[d, pl.ds(0, 24, stride=2), :] = up
            H1[d, pl.ds(1, 24, stride=2), :] = up

        arrive(to_mid)

        def keep_1(g, d, a, b):
            F1[d, 8 * g : 8 * g + 8, :] = a
            V1[d, 8 * g : 8 * g + 8, :] = b * masks[g]

        mid_whole(E2.at[cycle], R2.at[cycle], keep_1)
        c1, w1, big1, f1 = load(C1, 4), load(W1, 4), load(D1, 4), load(F1, 4)
        v1 = [V1[d] + H1[d // 2, 16:40, :] for d in range(4)]
        for _ in range(2):
            v1 = sweep(v1, f1, c1, w1, big1)
        for d in range(8):
            T[0, pl.ds(d, 24, stride=8), :] = v1[d // 2]

        near = lane // 2
        for q in range((9 - wide) // 2 + 2, (30 + wide) // 2 + 3):
            row = T[0, 8 * q : 8 * q + 8, :]
            up = [pick(row, near), pick(row, 64 + near)]
            for r in (2 * q - 4, 2 * q - 3):
                for t in range(2):
                    VA[t, r] = VB[t, r] + up[t]
        fine_sweep(source, rows_of(VA), 10 - wide, 30 + wide, put(VB))

        def add(t, q, v):
            K[t, q] = v if cycle == 0 else K[t, q] + v

        fine_sweep(source, rows_of(VB), 11 - wide, 29 + wide, add)

        def keep_residual(q, spread, flux):
            if final:
                v = K[0, q]
                out[pl.ds(q - OWN, DEPTH, stride=WIDE), :] = v
                res[pl.ds(q - OWN, DEPTH, stride=WIDE), :] = fine_change(q, 0, v, F.at[0], spread, flux)
            else:
                for t in range(2):
                    F[cycle + 1, t, q] = fine_change(q, t, K[t, q], F.at[0], spread, flux)

        blur_rows(rows_of(K), 12 - wide, 28 + wide, keep_residual)

    for c in ends:
        c.wait_send()


def per_device(gx_count, gy_count, rhs, cond_class, charge_class, cond_table, charge_table):
    flat = (DEPTH * WIDE, LONG)
    f32, i32 = jnp.float32, jnp.int32
    tile = (8, 128)
    fine = pltpu.VMEM((2, 40) + tile, f32)
    mid = pltpu.VMEM((4, 24, 128), f32)
    low = pltpu.VMEM((2, 48, 128), f32)
    scratch = [
        pltpu.VMEM(flat, f32), pltpu.VMEM(flat, i32), pltpu.VMEM(flat, i32), pltpu.SMEM((16,), f32), pltpu.SMEM((16,), f32),
        fine, fine, fine, pltpu.VMEM((CYCLES, 2, 40) + tile, f32), fine, fine, fine,
        pltpu.VMEM((2, 4) + tile, f32), pltpu.VMEM((2, 2, 10) + tile, f32), pltpu.VMEM((2, 192, 128), f32),
        mid, mid, mid, mid, mid,
        pltpu.VMEM((2,) + tile, f32), pltpu.VMEM((8, 2) + tile, f32),
        pltpu.VMEM((CYCLES, 4) + tile, f32), pltpu.VMEM((CYCLES, 8, 4) + tile, f32),
        pltpu.VMEM((2, 32, 128), f32), pltpu.VMEM((2, 16, 128), f32),
        pltpu.VMEM((2,) + tile, f32), pltpu.VMEM((2, 128), f32),
        pltpu.VMEM((len(AROUND),) + tile, f32), pltpu.VMEM((len(NEARER), 2, 128), f32),
        low, low, low, low, low, pltpu.VMEM((48, 128), f32),
        pltpu.VMEM((48, 128), f32), pltpu.VMEM((2, 48, 128), f32), pltpu.VMEM((3, 24, 128), f32),
        pltpu.SemaphoreType.DMA((COPIES,)), pltpu.SemaphoreType.DMA((COPIES,)), pltpu.SemaphoreType.DMA((5,)),
    ]
    hbm, vmem = pl.BlockSpec(memory_space=pl.ANY), pl.BlockSpec(memory_space=pltpu.VMEM)
    correction, residual = pl.pallas_call(
        functools.partial(kernel, gx_count, gy_count),
        out_shape=[pltpu.VMEM(flat, f32)] * 2,
        in_specs=[hbm] * 5,
        out_specs=[vmem, vmem],
        scratch_shapes=scratch,
        compiler_params=pltpu.CompilerParams(collective_id=0, has_side_effects=True),
    )(rhs.reshape(flat), cond_class.reshape(flat), charge_class.reshape(flat), cond_table, charge_table)
    return correction.reshape(rhs.shape), residual.reshape(rhs.shape)


def solution(mesh):
    placed = (P(None, "gx", "gy"), P(None, "gx", "gy"), P(None, "gx", "gy"), P(), P())
    return jax.shard_map(
        functools.partial(per_device, mesh.shape["gx"], mesh.shape["gy"]),
        mesh=mesh,
        in_specs=placed,
        out_specs=(P(None, "gx", "gy"), P(None, "gx", "gy")),
        check_vma=False,
    )
```

```python
import functools

import jax
import jax.numpy as jnp
from jax import lax
from jax.experimental import pallas as pl
from jax.experimental.pallas import tpu as pltpu
from jax.sharding import PartitionSpec as P

MESH = pl.DeviceIdType.MESH
CYCLES = 2
COARSE_SWEEPS = 6
RELAX = 0.9
SHIFT = 0.1
DEPTH, WIDE, LONG = 8, 16, 128
OWN = 12
SIDES = ((1, 0), (-1, 0), (0, 1), (0, -1), (1, 1), (1, -1), (-1, 1), (-1, -1))
AROUND = tuple((s * a, b) for b in (-1, 1, 0) for a in (5, 2, 3, 1, 4, 0) for s in ((1, -1) if a else (1,)) if a or b)
NEARER = tuple(p for p in AROUND if abs(p[0]) < 5)

FINE, FINE_MORE, MID, FAR = 0, 2, 4, 7
COPIES = 9


def roll(x, shift, axis):
    shift %= x.shape[axis]
    return pltpu.roll(x, shift, axis) if shift else x


def pick(x, index):
    return jnp.take_along_axis(x, index, axis=1)


def blur(fields):
    along = []
    for v in fields:
        y = (v + v) + (roll(v, 1, 1) + roll(v, -1, 1))
        along.append((y + y) + (roll(y, 1, 0) + roll(y, -1, 0)))
    if len(along) == 1:
        return along
    pairs = [along[0]] + [a + b for a, b in zip(along, along[1:])] + [along[-1]]
    return [a + b for a, b in zip(pairs, pairs[1:])]


def operate(v, c, big):
    spread = blur(v)
    flux = blur([a * b for a, b in zip(c, v)])
    return [g * a - (b * s + f) for g, a, b, s, f in zip(big, v, c, spread, flux)]


def sweep(v, f, c, w, big):
    return [a + q * (s - o) for a, q, s, o in zip(v, w, f, operate(v, c, big))]


def residual_of(v, f, c, big):
    return [s - o for s, o in zip(f, operate(v, c, big))]


def diagonal(c, level, scale):
    own = scale * (6.0 + SHIFT * 4.0**level)
    return [own * a + b for a, b in zip(c, blur(c))]


def weight(c, diag):
    return [jnp.where(a > 0.0, RELAX / jnp.where(a > 0.0, d, 1.0), 0.0) for a, d in zip(c, diag)]


def look_up(classes, table):
    bits = [(classes & (1 << b)) != 0 for b in range(4)]
    level = [table[i] for i in range(16)]
    for bit in bits:
        level = [jnp.where(bit, level[2 * i + 1], level[2 * i]) for i in range(len(level) // 2)]
    return level[0]


def kernel(gx_count, gy_count, rhs_in, cond_in, charge_in, cond_table_in, charge_table_in, out, res, *scratch):
    (rhs, cond, charge, cond_table, charge_table, C, W, D, F, VA, VB, K, PS, PR, T, C1, W1, D1, F1, V1, E1, R1, E2, R2, G, S2,
     AS, AL, BF, BL, C2, W2, D2, F2, V2, G3, H2, H1, Z, send_sem, recv_sem, in_sem) = scratch
    gx, gy = lax.axis_index("gx"), lax.axis_index("gy")

    def at(dx, dy):
        return (lax.rem(gx + (dx + gx_count), gx_count), lax.rem(gy + (dy + gy_count), gy_count))

    def copy(src, dst, number, where):
        return pltpu.make_async_remote_copy(
            src_ref=src, dst_ref=dst, send_sem=send_sem.at[number], recv_sem=recv_sem.at[number],
            device_id=where, device_id_type=MESH,
        )

    pairs = ((cond_table_in, cond_table), (charge_table_in, charge_table), (cond_in, cond), (charge_in, charge), (rhs_in, rhs))
    inputs = [pltpu.make_async_copy(a, b, in_sem.at[i]) for i, (a, b) in enumerate(pairs)]
    for c in inputs:
        c.start()
    barrier = pltpu.get_barrier_semaphore()
    for peer in AROUND:
        pl.semaphore_signal(barrier, inc=1, device_id=at(*peer), device_id_type=MESH)

    left_in, right_in = gy > 0, gy < gy_count - 1
    low_in = jnp.where(gx > 0, 1.0, 0.0)
    high_in = jnp.where(gx < gx_count - 1, 1.0, 0.0)
    lane = lax.broadcasted_iota(jnp.int32, (8, 128), 1)
    sub = lax.broadcasted_iota(jnp.int32, (8, 128), 0)
    lane24 = lax.broadcasted_iota(jnp.int32, (24, 128), 1)
    first, last = lane == 0, lane == 127
    above = jnp.where(sub == 0, 0.0, 0.5)
    below = jnp.where(sub == 7, 0.0, 0.5)
    yes_left = jnp.where(left_in, 1.0, 0.0)
    yes_right = jnp.where(right_in, 1.0, 0.0)


    def fine_copies(n, array, h):
        ends = (
            (array.at[0, pl.ds(28 - h, h)], array.at[0, pl.ds(12 - h, h)]),
            (array.at[0, pl.ds(12, h)], array.at[0, pl.ds(28, h)]),
            (PS.at[n], PR.at[n, 0, pl.ds(3, 4)]),
            (PS.at[n], PR.at[n, 1, pl.ds(3, 4)]),
            (PS.at[n, pl.ds(2, 2)], PR.at[n, 0, pl.ds(1, 2)]),
            (PS.at[n, pl.ds(2, 2)], PR.at[n, 1, pl.ds(1, 2)]),
            (PS.at[n, pl.ds(0, 2)], PR.at[n, 0, pl.ds(7, 2)]),
            (PS.at[n, pl.ds(0, 2)], PR.at[n, 1, pl.ds(7, 2)]),
        )
        return [copy(*ends[i], FINE + n, at(*SIDES[i])) for i in (4, 5, 6, 7, 0, 1, 2, 3)]

    def more_copies(n, array, h):
        ends = (
            (array.at[0, pl.ds(24 - h, 4)], array.at[0, pl.ds(8 - h, 4)], 0),
            (array.at[0, pl.ds(12 + h, 4)], array.at[0, pl.ds(28 + h, 4)], 1),
            (PS.at[n, 1], PR.at[n, 0, 0], 4),
            (PS.at[n, 1], PR.at[n, 1, 0], 5),
            (PS.at[n, 2], PR.at[n, 0, 9], 6),
            (PS.at[n, 2], PR.at[n, 1, 9], 7),
        )
        return [copy(a, b, FINE_MORE + n, at(*SIDES[k])) for i, (a, b, k) in enumerate(ends)]

    def pack_edges(n, array):
        for b in range(4):
            packed = None
            for i in range(4):
                row = roll(array[0, OWN + 4 * b + i], 32 * i + 16, 1)
                packed = row if packed is None else jnp.where(lane >= 32 * i, row, packed)
            PS[n, b] = packed

    def unpack_edges(n, array, blocks, lo, hi):
        from_left = lax.rem(lane, 32) < 16
        for b in blocks:
            packed = jnp.where(from_left, PR[n, 0, b], PR[n, 1, b])
            for i in range(4):
                if lo <= 4 * b + i < hi:
                    array[1, 4 * b + i] = roll(packed, -(32 * i + 16), 1)

    def blur_row(t0, t1):
        a0, a1, b0, b1 = roll(t0, 1, 1), roll(t1, 1, 1), roll(t0, -1, 1), roll(t1, -1, 1)
        y0 = (t0 + t0) + (jnp.where(first, a1, a0) + jnp.where(last, b1, b0))
        y1 = (t1 + t1) + (jnp.where(first, a0, a1) + jnp.where(last, b0, b1))
        return [y + (above * roll(y, 1, 0) + below * roll(y, -1, 0)) for y in (y0, y1)]

    def blur_rows(row, lo, hi, use, flux=True):
        before = pair = held_v = None
        for r in range(lo - 1, hi + 1):
            v = row(r)
            fields = [v, [C[t, r] * v[t] for t in range(2)]] if flux else [v]
            now = [blur_row(*f) for f in fields]
            if before is not None:
                two = [[a + b for a, b in zip(x, y)] for x, y in zip(before, now)]
                if pair is not None:
                    use(r - 1, held_v, *[[a + b for a, b in zip(x, y)] for x, y in zip(pair, two)])
                pair = two
            before, held_v = now, v

    def fine_change(q, t, v, f, spread, flux):
        return f[t, q] - (D[t, q] * v - (C[t, q] * spread[t] + flux[t]))

    def fine_sweep(source, row, lo, hi, keep):
        def use(q, v, spread, flux):
            for t in range(2):
                keep(t, q, v[t] + W[t, q] * fine_change(q, t, v[t], source, spread, flux))

        blur_rows(row, lo, hi, use)

    def rows_of(array):
        return lambda r: [array[0, r], array[1, r]]

    def put(array):
        def keep(t, q, v):
            array[t, q] = v

        return keep

    def mask_conductivity(rows):
        side = jnp.where(lane < 64, yes_right, yes_left)
        for r in rows:
            if OWN <= r < OWN + WIDE:
                C[1, r] = C[1, r] * side
            else:
                mask = low_in if r < OWN else high_in
                C[0, r] = C[0, r] * mask
                C[1, r] = C[1, r] * (side * mask)

    def coefficients(q, v, spread):
        for t in range(2):
            c = v[t]
            diag = (4.0 * (6.0 + SHIFT)) * c + spread[t]
            inside = c > 0.0
            D[t, q] = diag + 8.0 * c
            W[t, q] = jnp.where(inside, RELAX / jnp.where(inside, diag, 1.0), 0.0)

    def fine_pairs(t):
        return [T[t, pl.ds(2 * d, 24, stride=8), :] + T[t, pl.ds(2 * d + 1, 24, stride=8), :] for d in range(4)]

    twice = lax.rem(2 * lane24, 128)

    def along_pairs(v, index):
        return pick(v + roll(v, -1, 1), index)


    def two_in_one(a, b):
        return jnp.where(lane < 64, a, roll(b, 64, 1))

    def mid_copies(number, source, target):
        return [copy(source, target.at[i], number, at(*SIDES[i])) for i in (4, 5, 6, 7, 0, 1, 2, 3)]

    def mid_whole(own, arrived, keep):
        for g, (middle, before, after) in enumerate(((0, 4, 5), (None, 2, 3), (1, 6, 7))):
            for d in range(own.shape[0]):
                m = own[d] if middle is None else arrived[middle, d]
                outer = jnp.where(lane < 32, arrived[after, d], arrived[before, d])
                outer2 = jnp.where(lane < 96, arrived[after, d], arrived[before, d])
                keep(g, d, jnp.where(lane < 64, m, roll(outer, 64, 1)), jnp.where(lane < 64, roll(m, 64, 1), outer2))

    def stack_depth(a, b):
        return jnp.where(sub < 4, a, roll(b, 4, 0))


    spot = 2 * lax.rem(lane, 32)
    mid_side = jnp.where(lane < 64, 1.0, jnp.where(lane < 96, yes_right, yes_left))
    masks = (mid_side * low_in, mid_side, mid_side * high_in)

    def far_copies(n, source, target, peers):
        return [copy(source, target.at[i], FAR + n, at(*p)) for i, p in enumerate(peers)]

    def by_side(left, middle, right):
        return jnp.where(lane < 32, left, jnp.where(lane < 64, middle, right))

    def first_block(a):
        parts = [AS[0] if (a, b) == (0, 0) else BF[AROUND.index((-a, -b))] for b in (-1, 0, 1)]
        return [by_side(*[roll(v, 32 * (k - j), 1) for k, v in enumerate(parts)]) for j in range(3)]

    unfold = 32 * lax.rem(sub, 4) + lax.rem(lane, 32)

    def later_block(a):
        parts = []
        for b in (-1, 0, 1):
            if (a, b) == (0, 0):
                parts.append(AS[1])
            else:
                k = NEARER.index((-a, -b))
                rows = [jnp.broadcast_to(BL[k, d : d + 1, :], (8, 128)) for d in range(2)]
                parts.append(pick(jnp.where(sub < 4, *rows), unfold))
        return [by_side(*parts)]

    def spread_far(block, reach, arrays, mask):
        zero = jnp.zeros((8, 128), jnp.float32)
        for g in range(6):
            pair = []
            for a in (2 * g - 5, 2 * g - 4):
                blocks = block(a) if abs(a) <= reach else [zero] * len(arrays)
                if mask is not None and abs(a) <= reach:
                    there = jnp.where(jnp.logical_and(gx + a >= 0, gx + a < gx_count), 1.0, 0.0)
                    blocks[0] = blocks[0] * (mask * there)
                pair.append(blocks)
            for j, array in enumerate(arrays):
                array[0, 8 * g : 8 * g + 8, :] = stack_depth(pair[0][j], pair[1][j])
                array[1, 8 * g : 8 * g + 8, :] = jnp.where(sub < 4, roll(pair[0][j], 4, 0), pair[1][j])

    def load(ref, count):
        return [ref[d] for d in range(count)]

    ends = []

    def start(copies, group=None):
        for c in copies:
            c.start()
        if group is None:
            ends.extend(copies)
            return copies
        buffer, number = group
        whole = [copy(buffer, buffer, number, at(1, 0))]
        ends.extend(whole)
        return whole

    def arrive(copies):
        for c in copies:
            c.wait_recv()

    T[...] = jnp.zeros_like(T)
    G[...] = jnp.zeros_like(G)
    for c in inputs:
        c.wait()
    for x in range(WIDE):
        where = pl.ds(x, DEPTH, stride=WIDE)
        lost = 1.0 - look_up(charge[where, :], charge_table)
        C[0, OWN + x] = (look_up(cond[where, :], cond_table) * 0.25) * lost
        F[0, 0, OWN + x] = rhs[where, :]
    pack_edges(0, C)
    pack_edges(1, F.at[0])
    for q in range(8, 16):
        r = 2 * q - 4
        T[0, 8 * q : 8 * q + 8, :] = C[0, r] + C[0, r + 1]
    own = [along_pairs(v, twice)[8:16] * (0.125 * 0.125) for v in fine_pairs(0)]
    for d in range(2):
        E1[d] = two_in_one(own[d], own[d + 2])

    pl.semaphore_wait(barrier, len(AROUND))
    to_c = start(fine_copies(0, C, 7), (C.at[0, pl.ds(0, 30)], FINE))
    to_f = start(fine_copies(1, F.at[0], 6), (F.at[0, 0, pl.ds(0, 28)], FINE + 1))
    to_c1 = start(mid_copies(MID, E1, R1), (R1, MID))
    to_more = start(more_copies(0, C, 7), (C.at[0, pl.ds(0, 12)], FINE_MORE))
    to_more += start(more_copies(1, F.at[0], 6), (F.at[0, 0, pl.ds(0, 12)], FINE_MORE + 1))

    arrive(to_c)
    unpack_edges(0, C, range(1, 9), 5, 35)
    mask_conductivity(range(5, 35))
    blur_rows(rows_of(C), 6, 34, coefficients, flux=False)

    for cycle in range(CYCLES):
        source = F.at[cycle]
        final = cycle + 1 == CYCLES
        wide = 0 if final else 6

        if cycle == 0:
            arrive(to_f)
            unpack_edges(1, source, range(1, 9), 6, 34)

        def scaled(r):
            return [W[t, r] * source[t, r] for t in range(2)]

        fine_sweep(source, scaled, 7, 33, put(VB))
        held = {}

        def pair_up(q, v, spread, flux):
            for t in range(2):
                change = fine_change(q, t, v[t], source, spread, flux)
                if q % 2 == 0:
                    held[t] = change
                else:
                    at_row = 8 * (2 + q // 2)
                    T[t, at_row : at_row + 8, :] = held[t] + change

        blur_rows(rows_of(VB), 8, 32, pair_up)
        for d, (v0, v1) in enumerate(zip(fine_pairs(0), fine_pairs(1))):
            F1[d] = jnp.where(lane24 < 64, along_pairs(v0, twice), along_pairs(v1, twice)) * 0.125

        if cycle == 0:
            arrive(to_c1)

            def keep_c1(g, d, a, b):
                C1[d, 8 * g : 8 * g + 8, :] = a * masks[g]
                C1[d + 2, 8 * g : 8 * g + 8, :] = b * masks[g]

            mid_whole(E1, R1, keep_c1)
            c1 = load(C1, 4)
            diag = diagonal(c1, 1, 8.0)
            for d, w in enumerate(weight(c1, diag)):
                W1[d] = w
                D1[d] = diag[d] + 16.0 * c1[d]
            for d in range(2):
                G[d, 0:24, :] = c1[2 * d] + c1[2 * d + 1]
            c2 = []
            own_c = []
            for d in range(2):
                pairs = G[d, pl.ds(0, 16, stride=2), :] + G[d, pl.ds(1, 16, stride=2), :]
                c2.append(along_pairs(pairs, twice[:16]) * (0.125 * 0.25))
                pairs = G[d, pl.ds(8, 8, stride=2), :] + G[d, pl.ds(9, 8, stride=2), :]
                own_c.append(along_pairs(pairs, spot) * (0.125 * 0.25))
            own_d = []
            for d, v in enumerate(diagonal(c2, 2, 8.0)):
                S2[d] = v
                own_d.append(pick(S2[d, 4:12, :], spot // 2))

        c1, w1, big1 = load(C1, 4), load(W1, 4), load(D1, 4)
        f1 = load(F1, 4)
        v1 = sweep([w * f for w, f in zip(w1, f1)], f1, c1, w1, big1)
        r1 = residual_of(v1, f1, c1, big1)
        own = []
        for d in range(2):
            G[d, 0:24, :] = r1[2 * d] + r1[2 * d + 1]
            pairs = G[d, pl.ds(8, 8, stride=2), :] + G[d, pl.ds(9, 8, stride=2), :]
            own.append(along_pairs(pairs, spot) * 0.125)
        own = stack_depth(*own)
        if cycle == 0:
            AS[0] = jnp.where(lane < 32, stack_depth(*own_c), jnp.where(lane < 64, stack_depth(*own_d), own))
            to_far = start(far_copies(0, AS.at[0], BF, AROUND), (BF, FAR))
        else:
            AS[1] = own
            one = jnp.where(lane // 32 == lax.rem(sub, 4), own, 0.0)
            one = one + roll(one, -1, 0)
            one = one + roll(one, -2, 0)
            AL[...] = jnp.where(sub == 0, one, roll(one, -3, 0))[0:2]
            to_far = start(far_copies(1, AL, BL, NEARER), (BL, FAR + 1))

        def send_mid():
            return start(mid_copies(MID + 1 + cycle, E2.at[cycle], R2.at[cycle]), (R2.at[cycle], MID + 1 + cycle))

        for d in range(4):
            V1[d] = v1[d]
            E2[cycle, d] = two_in_one(F1[d, 8:16, :], V1[d, 8:16, :])
        to_mid = send_mid()

        if cycle == 0:
            arrive(to_more)
            unpack_edges(0, C, (0, 1, 8, 9), 1, 5)
            unpack_edges(0, C, (8, 9), 35, 39)
            unpack_edges(1, source, (0, 1), 2, 6)
            unpack_edges(1, source, (8, 9), 34, 38)
            mask_conductivity([*range(1, 5), *range(35, 39)])
            blur_rows(rows_of(C), 2, 6, coefficients, flux=False)
            blur_rows(rows_of(C), 34, 38, coefficients, flux=False)
            fine_sweep(source, scaled, 3, 7, put(VB))
            fine_sweep(source, scaled, 33, 37, put(VB))

        arrive(to_far)
        if cycle == 0:
            side = jnp.where(lane < 32, yes_left, jnp.where(lane < 64, 1.0, yes_right))
            spread_far(first_block, 5, (C2, D2, F2), side)
            c2 = load(C2, 2)
            diag = load(D2, 2)
            for d, w in enumerate(weight(c2, diag)):
                W2[d] = w
                D2[d] = diag[d] + 16.0 * c2[d]
        else:
            spread_far(later_block, 4, (F2,), None)
        c2, w2, big2, f2 = load(C2, 2), load(W2, 2), load(D2, 2), load(F2, 2)
        v2 = sweep([w * f for w, f in zip(w2, f2)], f2, c2, w2, big2)
        for d in range(2):
            V2[d] = v2[d]
        r2 = residual_of(v2, f2, c2, big2)
        if cycle == 0:
            G3[...] = c2[0] + c2[1]
            pairs = G3[pl.ds(0, 24, stride=2), :] + G3[pl.ds(1, 24, stride=2), :]
            c3 = [along_pairs(pairs, twice) * (0.125 * 0.5)]
            diag = diagonal(c3, 3, 4.0)
            w3 = weight(c3, diag)
            big3 = [diag[0] + 8.0 * c3[0]]
            for j, v in enumerate((c3, w3, big3)):
                Z[j] = v[0]
        H2[...] = r2[0] + r2[1]

        pairs = H2[pl.ds(0, 24, stride=2), :] + H2[pl.ds(1, 24, stride=2), :]
        f3 = [along_pairs(pairs, twice) * 0.125]
        c3, w3, big3 = [Z[0]], [Z[1]], [Z[2]]
        v3 = [w3[0] * f3[0]]
        for _ in range(COARSE_SWEEPS - 1):
            v3 = sweep(v3, f3, c3, w3, big3)
        half = lane24 // 2
        up = pick(v3[0], half)
        H2[pl.ds(0, 24, stride=2), :] = up
        H2[pl.ds(1, 24, stride=2), :] = up

        c2, w2, big2, f2 = [[ref[d, 8:32, :] for d in range(2)] for ref in (C2, W2, D2, F2)]
        v2 = [V2[d, 8:32, :] + H2[8:32, :] for d in range(2)]
        for _ in range(2):
            v2 = sweep(v2, f2, c2, w2, big2)
        down = jnp.where(lane24 < 96, 32 + half, half - 32)
        for d in range(2):
            up = pick(v2[d], down)
            H1[d, pl.ds(0, 24, stride=2), :] = up
            H1[d, pl.ds(1, 24, stride=2), :] = up

        arrive(to_mid)

        def keep_1(g, d, a, b):
            F1[d, 8 * g : 8 * g + 8, :] = a
            V1[d, 8 * g : 8 * g + 8, :] = b * masks[g]

        mid_whole(E2.at[cycle], R2.at[cycle], keep_1)
        c1, w1, big1, f1 = load(C1, 4), load(W1, 4), load(D1, 4), load(F1, 4)
        v1 = [V1[d] + H1[d // 2, 16:40, :] for d in range(4)]
        for _ in range(2):
            v1 = sweep(v1, f1, c1, w1, big1)
        for d in range(8):
            T[0, pl.ds(d, 24, stride=8), :] = v1[d // 2]

        near = lane // 2
        for q in range((9 - wide) // 2 + 2, (30 + wide) // 2 + 3):
            row = T[0, 8 * q : 8 * q + 8, :]
            up = [pick(row, near), pick(row, 64 + near)]
            for r in (2 * q - 4, 2 * q - 3):
                for t in range(2):
                    VA[t, r] = VB[t, r] + up[t]
        fine_sweep(source, rows_of(VA), 10 - wide, 30 + wide, put(VB))

        def add(t, q, v):
            K[t, q] = v if cycle == 0 else K[t, q] + v

        fine_sweep(source, rows_of(VB), 11 - wide, 29 + wide, add)

        def keep_residual(q, v, spread, flux):
            if final:
                out[pl.ds(q - OWN, DEPTH, stride=WIDE), :] = v[0]
                res[pl.ds(q - OWN, DEPTH, stride=WIDE), :] = fine_change(q, 0, v[0], F.at[0], spread, flux)
            else:
                for t in range(2):
                    F[cycle + 1, t, q] = fine_change(q, t, v[t], F.at[0], spread, flux)

        blur_rows(rows_of(K), 12 - wide, 28 + wide, keep_residual)

    for c in ends:
        c.wait_send()


def per_device(gx_count, gy_count, rhs, cond_class, charge_class, cond_table, charge_table):
    flat = (DEPTH * WIDE, LONG)
    f32, i32 = jnp.float32, jnp.int32
    tile = (8, 128)
    fine = pltpu.VMEM((2, 40) + tile, f32)
    mid = pltpu.VMEM((4, 24, 128), f32)
    low = pltpu.VMEM((2, 48, 128), f32)
    scratch = [
        pltpu.VMEM(flat, f32), pltpu.VMEM(flat, i32), pltpu.VMEM(flat, i32), pltpu.SMEM((16,), f32), pltpu.SMEM((16,), f32),
        fine, fine, fine, pltpu.VMEM((CYCLES, 2, 40) + tile, f32), fine, fine, fine,
        pltpu.VMEM((2, 4) + tile, f32), pltpu.VMEM((2, 2, 10) + tile, f32), pltpu.VMEM((2, 192, 128), f32),
        mid, mid, mid, mid, mid,
        pltpu.VMEM((2,) + tile, f32), pltpu.VMEM((8, 2) + tile, f32),
        pltpu.VMEM((CYCLES, 4) + tile, f32), pltpu.VMEM((CYCLES, 8, 4) + tile, f32),
        pltpu.VMEM((2, 32, 128), f32), pltpu.VMEM((2, 16, 128), f32),
        pltpu.VMEM((2,) + tile, f32), pltpu.VMEM((2, 128), f32),
        pltpu.VMEM((len(AROUND),) + tile, f32), pltpu.VMEM((len(NEARER), 2, 128), f32),
        low, low, low, low, low, pltpu.VMEM((48, 128), f32),
        pltpu.VMEM((48, 128), f32), pltpu.VMEM((2, 48, 128), f32), pltpu.VMEM((3, 24, 128), f32),
        pltpu.SemaphoreType.DMA((COPIES,)), pltpu.SemaphoreType.DMA((COPIES,)), pltpu.SemaphoreType.DMA((5,)),
    ]
    hbm, vmem = pl.BlockSpec(memory_space=pl.ANY), pl.BlockSpec(memory_space=pltpu.VMEM)
    correction, residual = pl.pallas_call(
        functools.partial(kernel, gx_count, gy_count),
        out_shape=[pltpu.VMEM(flat, f32)] * 2,
        in_specs=[hbm] * 5,
        out_specs=[vmem, vmem],
        scratch_shapes=scratch,
        compiler_params=pltpu.CompilerParams(collective_id=0, has_side_effects=True),
    )(rhs.reshape(flat), cond_class.reshape(flat), charge_class.reshape(flat), cond_table, charge_table)
    return correction.reshape(rhs.shape), residual.reshape(rhs.shape)


def solution(mesh):
    placed = (P(None, "gx", "gy"), P(None, "gx", "gy"), P(None, "gx", "gy"), P(), P())
    return jax.shard_map(
        functools.partial(per_device, mesh.shape["gx"], mesh.shape["gy"]),
        mesh=mesh,
        in_specs=placed,
        out_specs=(P(None, "gx", "gy"), P(None, "gx", "gy")),
        check_vma=False,
    )
```

```python
import functools

import jax
import jax.numpy as jnp
from jax import lax
from jax.experimental import pallas as pl
from jax.experimental.pallas import tpu as pltpu
from jax.sharding import PartitionSpec as P

MESH = pl.DeviceIdType.MESH
CYCLES = 2
COARSE_SWEEPS = 6
RELAX = 0.9
SHIFT = 0.1
DEPTH, WIDE, LONG = 8, 16, 128
OWN = 12
SIDES = ((1, 0), (-1, 0), (0, 1), (0, -1), (1, 1), (1, -1), (-1, 1), (-1, -1))
AROUND = tuple((s * a, b) for b in (-1, 1, 0) for a in (5, 2, 3, 1, 4, 0) for s in ((1, -1) if a else (1,)) if a or b)
NEARER = tuple(p for p in AROUND if abs(p[0]) < 5)

FINE, FINE_MORE, MID, FAR = 0, 2, 4, 7
COPIES = 9


def roll(x, shift, axis):
    shift %= x.shape[axis]
    return pltpu.roll(x, shift, axis) if shift else x


def pick(x, index):
    return jnp.take_along_axis(x, index, axis=1)


def blur(fields):
    along = []
    for v in fields:
        y = (v + v) + (roll(v, 1, 1) + roll(v, -1, 1))
        along.append((y + y) + (roll(y, 1, 0) + roll(y, -1, 0)))
    if len(along) == 1:
        return along
    pairs = [along[0]] + [a + b for a, b in zip(along, along[1:])] + [along[-1]]
    return [a + b for a, b in zip(pairs, pairs[1:])]


def operate(v, c, big):
    spread = blur(v)
    flux = blur([a * b for a, b in zip(c, v)])
    return [g * a - (b * s + f) for g, a, b, s, f in zip(big, v, c, spread, flux)]


def sweep(v, f, c, w, big):
    return [a + q * (s - o) for a, q, s, o in zip(v, w, f, operate(v, c, big))]


def residual_of(v, f, c, big):
    return [s - o for s, o in zip(f, operate(v, c, big))]


def diagonal(c, level, scale):
    own = scale * (6.0 + SHIFT * 4.0**level)
    return [own * a + b for a, b in zip(c, blur(c))]


def weight(c, diag):
    return [jnp.where(a > 0.0, RELAX / jnp.where(a > 0.0, d, 1.0), 0.0) for a, d in zip(c, diag)]


def look_up(classes, table):
    bits = [(classes & (1 << b)) != 0 for b in range(4)]
    level = [table[i] for i in range(16)]
    for bit in bits:
        level = [jnp.where(bit, level[2 * i + 1], level[2 * i]) for i in range(len(level) // 2)]
    return level[0]


def kernel(gx_count, gy_count, rhs_in, cond_in, charge_in, cond_table_in, charge_table_in, out, res, *scratch):
    (rhs, cond, charge, cond_table, charge_table, C, W, D, F, VA, VB, K, PS, PR, T, C1, W1, D1, F1, V1, E1, R1, E2, R2, G, S2,
     AS, AL, BF, BL, C2, W2, D2, F2, V2, G3, H2, H1, Z, send_sem, recv_sem, in_sem) = scratch
    gx, gy = lax.axis_index("gx"), lax.axis_index("gy")

    def at(dx, dy):
        return (lax.rem(gx + (dx + gx_count), gx_count), lax.rem(gy + (dy + gy_count), gy_count))

    def copy(src, dst, number, where):
        return pltpu.make_async_remote_copy(
            src_ref=src, dst_ref=dst, send_sem=send_sem.at[number], recv_sem=recv_sem.at[number],
            device_id=where, device_id_type=MESH,
        )

    pairs = ((cond_table_in, cond_table), (charge_table_in, charge_table), (cond_in, cond), (charge_in, charge), (rhs_in, rhs))
    inputs = [pltpu.make_async_copy(a, b, in_sem.at[i]) for i, (a, b) in enumerate(pairs)]
    for c in inputs:
        c.start()
    barrier = pltpu.get_barrier_semaphore()
    for peer in AROUND[::-1]:
        pl.semaphore_signal(barrier, inc=1, device_id=at(*peer), device_id_type=MESH)

    left_in, right_in = gy > 0, gy < gy_count - 1
    low_in = jnp.where(gx > 0, 1.0, 0.0)
    high_in = jnp.where(gx < gx_count - 1, 1.0, 0.0)
    lane = lax.broadcasted_iota(jnp.int32, (8, 128), 1)
    sub = lax.broadcasted_iota(jnp.int32, (8, 128), 0)
    lane24 = lax.broadcasted_iota(jnp.int32, (24, 128), 1)
    first, last = lane == 0, lane == 127
    above = jnp.where(sub == 0, 0.0, 0.5)
    below = jnp.where(sub == 7, 0.0, 0.5)
    yes_left = jnp.where(left_in, 1.0, 0.0)
    yes_right = jnp.where(right_in, 1.0, 0.0)


    def fine_copies(n, array, h):
        ends = (
            (array.at[0, pl.ds(28 - h, h)], array.at[0, pl.ds(12 - h, h)]),
            (array.at[0, pl.ds(12, h)], array.at[0, pl.ds(28, h)]),
            (PS.at[n], PR.at[n, 0, pl.ds(3, 4)]),
            (PS.at[n], PR.at[n, 1, pl.ds(3, 4)]),
            (PS.at[n, pl.ds(2, 2)], PR.at[n, 0, pl.ds(1, 2)]),
            (PS.at[n, pl.ds(2, 2)], PR.at[n, 1, pl.ds(1, 2)]),
            (PS.at[n, pl.ds(0, 2)], PR.at[n, 0, pl.ds(7, 2)]),
            (PS.at[n, pl.ds(0, 2)], PR.at[n, 1, pl.ds(7, 2)]),
        )
        return [copy(*ends[i], FINE + n, at(*SIDES[i])) for i in (4, 5, 6, 7, 0, 1, 2, 3)]

    def more_copies(n, array, h):
        ends = (
            (array.at[0, pl.ds(24 - h, 4)], array.at[0, pl.ds(8 - h, 4)], 0),
            (array.at[0, pl.ds(12 + h, 4)], array.at[0, pl.ds(28 + h, 4)], 1),
            (PS.at[n, 1], PR.at[n, 0, 0], 4),
            (PS.at[n, 1], PR.at[n, 1, 0], 5),
            (PS.at[n, 2], PR.at[n, 0, 9], 6),
            (PS.at[n, 2], PR.at[n, 1, 9], 7),
        )
        return [copy(a, b, FINE_MORE + n, at(*SIDES[k])) for i, (a, b, k) in enumerate(ends)]

    def pack_edges(n, array):
        for b in range(4):
            packed = None
            for i in range(4):
                row = roll(array[0, OWN + 4 * b + i], 32 * i + 16, 1)
                packed = row if packed is None else jnp.where(lane >= 32 * i, row, packed)
            PS[n, b] = packed

    def unpack_edges(n, array, blocks, lo, hi):
        from_left = lax.rem(lane, 32) < 16
        for b in blocks:
            packed = jnp.where(from_left, PR[n, 0, b], PR[n, 1, b])
            for i in range(4):
                if lo <= 4 * b + i < hi:
                    array[1, 4 * b + i] = roll(packed, -(32 * i + 16), 1)

    def blur_row(t0, t1):
        a0, a1, b0, b1 = roll(t0, 1, 1), roll(t1, 1, 1), roll(t0, -1, 1), roll(t1, -1, 1)
        y0 = (t0 + t0) + (jnp.where(first, a1, a0) + jnp.where(last, b1, b0))
        y1 = (t1 + t1) + (jnp.where(first, a0, a1) + jnp.where(last, b0, b1))
        return [y + (above * roll(y, 1, 0) + below * roll(y, -1, 0)) for y in (y0, y1)]

    def blur_rows(row, lo, hi, use, flux=True):
        before = pair = None
        for r in range(lo - 1, hi + 1):
            v = row(r)
            fields = [v, [C[t, r] * v[t] for t in range(2)]] if flux else [v]
            now = [blur_row(*f) for f in fields]
            if before is not None:
                two = [[a + b for a, b in zip(x, y)] for x, y in zip(before, now)]
                if pair is not None:
                    use(r - 1, *[[a + b for a, b in zip(x, y)] for x, y in zip(pair, two)])
                pair = two
            before = now

    def fine_change(q, t, v, f, spread, flux):
        return f[t, q] - (D[t, q] * v - (C[t, q] * spread[t] + flux[t]))

    def fine_sweep(source, row, lo, hi, keep):
        def use(q, spread, flux):
            v = row(q)
            for t in range(2):
                keep(t, q, v[t] + W[t, q] * fine_change(q, t, v[t], source, spread, flux))

        blur_rows(row, lo, hi, use)

    def rows_of(array):
        return lambda r: [array[0, r], array[1, r]]

    def put(array):
        def keep(t, q, v):
            array[t, q] = v

        return keep

    def mask_conductivity(rows):
        side = jnp.where(lane < 64, yes_right, yes_left)
        for r in rows:
            if OWN <= r < OWN + WIDE:
                C[1, r] = C[1, r] * side
            else:
                mask = low_in if r < OWN else high_in
                C[0, r] = C[0, r] * mask
                C[1, r] = C[1, r] * (side * mask)

    def coefficients(q, spread):
        for t in range(2):
            c = C[t, q]
            diag = (4.0 * (6.0 + SHIFT)) * c + spread[t]
            inside = c > 0.0
            D[t, q] = diag + 8.0 * c
            W[t, q] = jnp.where(inside, RELAX / jnp.where(inside, diag, 1.0), 0.0)

    def fine_pairs(t):
        return [T[t, pl.ds(2 * d, 24, stride=8), :] + T[t, pl.ds(2 * d + 1, 24, stride=8), :] for d in range(4)]

    twice = lax.rem(2 * lane24, 128)

    def along_pairs(v, index):
        return pick(v + roll(v, -1, 1), index)


    def two_in_one(a, b):
        return jnp.where(lane < 64, a, roll(b, 64, 1))

    def mid_copies(number, source, target):
        return [copy(source, target.at[i], number, at(*SIDES[i])) for i in (4, 5, 6, 7, 0, 1, 2, 3)]

    def mid_whole(own, arrived, keep):
        for g, (middle, before, after) in enumerate(((0, 4, 5), (None, 2, 3), (1, 6, 7))):
            for d in range(own.shape[0]):
                m = own[d] if middle is None else arrived[middle, d]
                outer = jnp.where(lane < 32, arrived[after, d], arrived[before, d])
                outer2 = jnp.where(lane < 96, arrived[after, d], arrived[before, d])
                keep(g, d, jnp.where(lane < 64, m, roll(outer, 64, 1)), jnp.where(lane < 64, roll(m, 64, 1), outer2))

    def stack_depth(a, b):
        return jnp.where(sub < 4, a, roll(b, 4, 0))


    spot = 2 * lax.rem(lane, 32)
    mid_side = jnp.where(lane < 64, 1.0, jnp.where(lane < 96, yes_right, yes_left))
    masks = (mid_side * low_in, mid_side, mid_side * high_in)

    def far_copies(n, source, target, peers):
        return [copy(source, target.at[i], FAR + n, at(*p)) for i, p in enumerate(peers)]

    def by_side(left, middle, right):
        return jnp.where(lane < 32, left, jnp.where(lane < 64, middle, right))

    def first_block(a):
        parts = [AS[0] if (a, b) == (0, 0) else BF[AROUND.index((-a, -b))] for b in (-1, 0, 1)]
        return [by_side(*[roll(v, 32 * (k - j), 1) for k, v in enumerate(parts)]) for j in range(3)]

    unfold = 32 * lax.rem(sub, 4) + lax.rem(lane, 32)

    def later_block(a):
        parts = []
        for b in (-1, 0, 1):
            if (a, b) == (0, 0):
                parts.append(AS[1])
            else:
                k = NEARER.index((-a, -b))
                rows = [jnp.broadcast_to(BL[k, d : d + 1, :], (8, 128)) for d in range(2)]
                parts.append(pick(jnp.where(sub < 4, *rows), unfold))
        return [by_side(*parts)]

    def spread_far(block, reach, arrays, mask):
        zero = jnp.zeros((8, 128), jnp.float32)
        for g in range(6):
            pair = []
            for a in (2 * g - 5, 2 * g - 4):
                blocks = block(a) if abs(a) <= reach else [zero] * len(arrays)
                if mask is not None and abs(a) <= reach:
                    there = jnp.where(jnp.logical_and(gx + a >= 0, gx + a < gx_count), 1.0, 0.0)
                    blocks[0] = blocks[0] * (mask * there)
                pair.append(blocks)
            for j, array in enumerate(arrays):
                array[0, 8 * g : 8 * g + 8, :] = stack_depth(pair[0][j], pair[1][j])
                array[1, 8 * g : 8 * g + 8, :] = jnp.where(sub < 4, roll(pair[0][j], 4, 0), pair[1][j])

    def load(ref, count):
        return [ref[d] for d in range(count)]

    ends = []

    def start(copies, group=None):
        for c in copies:
            c.start()
        if group is None:
            ends.extend(copies)
            return copies
        buffer, number = group
        whole = [copy(buffer, buffer, number, at(1, 0))]
        ends.extend(whole)
        return whole

    def arrive(copies):
        for c in copies:
            c.wait_recv()

    T[...] = jnp.zeros_like(T)
    G[...] = jnp.zeros_like(G)
    for c in inputs:
        c.wait()
    for x in range(WIDE):
        where = pl.ds(x, DEPTH, stride=WIDE)
        lost = 1.0 - look_up(charge[where, :], charge_table)
        C[0, OWN + x] = (look_up(cond[where, :], cond_table) * 0.25) * lost
        F[0, 0, OWN + x] = rhs[where, :]
    pack_edges(0, C)
    pack_edges(1, F.at[0])
    for q in range(8, 16):
        r = 2 * q - 4
        T[0, 8 * q : 8 * q + 8, :] = C[0, r] + C[0, r + 1]
    own = [along_pairs(v, twice)[8:16] * (0.125 * 0.125) for v in fine_pairs(0)]
    for d in range(2):
        E1[d] = two_in_one(own[d], own[d + 2])

    pl.semaphore_wait(barrier, len(AROUND))
    to_c = start(fine_copies(0, C, 7), (C.at[0, pl.ds(0, 30)], FINE))
    to_f = start(fine_copies(1, F.at[0], 6), (F.at[0, 0, pl.ds(0, 28)], FINE + 1))
    to_c1 = start(mid_copies(MID, E1, R1), (R1, MID))
    to_more = start(more_copies(0, C, 7), (C.at[0, pl.ds(0, 12)], FINE_MORE))
    to_more += start(more_copies(1, F.at[0], 6), (F.at[0, 0, pl.ds(0, 12)], FINE_MORE + 1))

    arrive(to_c)
    unpack_edges(0, C, range(1, 9), 5, 35)
    mask_conductivity(range(5, 35))
    blur_rows(rows_of(C), 6, 34, coefficients, flux=False)

    for cycle in range(CYCLES):
        source = F.at[cycle]
        final = cycle + 1 == CYCLES
        wide = 0 if final else 6

        if cycle == 0:
            arrive(to_f)
            unpack_edges(1, source, range(1, 9), 6, 34)

        def scaled(r):
            return [W[t, r] * source[t, r] for t in range(2)]

        fine_sweep(source, scaled, 7, 33, put(VB))
        held = {}

        def pair_up(q, spread, flux):
            v = [VB[0, q], VB[1, q]]
            for t in range(2):
                change = fine_change(q, t, v[t], source, spread, flux)
                if q % 2 == 0:
                    held[t] = change
                else:
                    at_row = 8 * (2 + q // 2)
                    T[t, at_row : at_row + 8, :] = held[t] + change

        blur_rows(rows_of(VB), 8, 32, pair_up)
        for d, (v0, v1) in enumerate(zip(fine_pairs(0), fine_pairs(1))):
            F1[d] = jnp.where(lane24 < 64, along_pairs(v0, twice), along_pairs(v1, twice)) * 0.125

        if cycle == 0:
            arrive(to_c1)

            def keep_c1(g, d, a, b):
                C1[d, 8 * g : 8 * g + 8, :] = a * masks[g]
                C1[d + 2, 8 * g : 8 * g + 8, :] = b * masks[g]

            mid_whole(E1, R1, keep_c1)
            c1 = load(C1, 4)
            diag = diagonal(c1, 1, 8.0)
            for d, w in enumerate(weight(c1, diag)):
                W1[d] = w
                D1[d] = diag[d] + 16.0 * c1[d]
            for d in range(2):
                G[d, 0:24, :] = c1[2 * d] + c1[2 * d + 1]
            c2 = []
            own_c = []
            for d in range(2):
                pairs = G[d, pl.ds(0, 16, stride=2), :] + G[d, pl.ds(1, 16, stride=2), :]
                c2.append(along_pairs(pairs, twice[:16]) * (0.125 * 0.25))
                pairs = G[d, pl.ds(8, 8, stride=2), :] + G[d, pl.ds(9, 8, stride=2), :]
                own_c.append(along_pairs(pairs, spot) * (0.125 * 0.25))
            own_d = []
            for d, v in enumerate(diagonal(c2, 2, 8.0)):
                S2[d] = v
                own_d.append(pick(S2[d, 4:12, :], spot // 2))

        c1, w1, big1 = load(C1, 4), load(W1, 4), load(D1, 4)
        f1 = load(F1, 4)
        v1 = sweep([w * f for w, f in zip(w1, f1)], f1, c1, w1, big1)
        r1 = residual_of(v1, f1, c1, big1)
        own = []
        for d in range(2):
            G[d, 0:24, :] = r1[2 * d] + r1[2 * d + 1]
            pairs = G[d, pl.ds(8, 8, stride=2), :] + G[d, pl.ds(9, 8, stride=2), :]
            own.append(along_pairs(pairs, spot) * 0.125)
        own = stack_depth(*own)
        if cycle == 0:
            AS[0] = jnp.where(lane < 32, stack_depth(*own_c), jnp.where(lane < 64, stack_depth(*own_d), own))
            to_far = start(far_copies(0, AS.at[0], BF, AROUND), (BF, FAR))
        else:
            AS[1] = own
            one = jnp.where(lane // 32 == lax.rem(sub, 4), own, 0.0)
            one = one + roll(one, -1, 0)
            one = one + roll(one, -2, 0)
            AL[...] = jnp.where(sub == 0, one, roll(one, -3, 0))[0:2]
            to_far = start(far_copies(1, AL, BL, NEARER), (BL, FAR + 1))

        def send_mid():
            return start(mid_copies(MID + 1 + cycle, E2.at[cycle], R2.at[cycle]), (R2.at[cycle], MID + 1 + cycle))

        for d in range(4):
            V1[d] = v1[d]
            E2[cycle, d] = two_in_one(F1[d, 8:16, :], V1[d, 8:16, :])
        to_mid = send_mid()

        if cycle == 0:
            arrive(to_more)
            unpack_edges(0, C, (0, 1, 8, 9), 1, 5)
            unpack_edges(0, C, (8, 9), 35, 39)
            unpack_edges(1, source, (0, 1), 2, 6)
            unpack_edges(1, source, (8, 9), 34, 38)
            mask_conductivity([*range(1, 5), *range(35, 39)])
            blur_rows(rows_of(C), 2, 6, coefficients, flux=False)
            blur_rows(rows_of(C), 34, 38, coefficients, flux=False)
            fine_sweep(source, scaled, 3, 7, put(VB))
            fine_sweep(source, scaled, 33, 37, put(VB))

        arrive(to_far)
        if cycle == 0:
            side = jnp.where(lane < 32, yes_left, jnp.where(lane < 64, 1.0, yes_right))
            spread_far(first_block, 5, (C2, D2, F2), side)
            c2 = load(C2, 2)
            diag = load(D2, 2)
            for d, w in enumerate(weight(c2, diag)):
                W2[d] = w
                D2[d] = diag[d] + 16.0 * c2[d]
        else:
            spread_far(later_block, 4, (F2,), None)
        c2, w2, big2, f2 = load(C2, 2), load(W2, 2), load(D2, 2), load(F2, 2)
        v2 = sweep([w * f for w, f in zip(w2, f2)], f2, c2, w2, big2)
        for d in range(2):
            V2[d] = v2[d]
        r2 = residual_of(v2, f2, c2, big2)
        if cycle == 0:
            G3[...] = c2[0] + c2[1]
            pairs = G3[pl.ds(0, 24, stride=2), :] + G3[pl.ds(1, 24, stride=2), :]
            c3 = [along_pairs(pairs, twice) * (0.125 * 0.5)]
            diag = diagonal(c3, 3, 4.0)
            w3 = weight(c3, diag)
            big3 = [diag[0] + 8.0 * c3[0]]
            for j, v in enumerate((c3, w3, big3)):
                Z[j] = v[0]
        H2[...] = r2[0] + r2[1]

        pairs = H2[pl.ds(0, 24, stride=2), :] + H2[pl.ds(1, 24, stride=2), :]
        f3 = [along_pairs(pairs, twice) * 0.125]
        c3, w3, big3 = [Z[0]], [Z[1]], [Z[2]]
        v3 = [w3[0] * f3[0]]
        for _ in range(COARSE_SWEEPS - 1):
            v3 = sweep(v3, f3, c3, w3, big3)
        half = lane24 // 2
        up = pick(v3[0], half)
        H2[pl.ds(0, 24, stride=2), :] = up
        H2[pl.ds(1, 24, stride=2), :] = up

        c2, w2, big2, f2 = [[ref[d, 8:32, :] for d in range(2)] for ref in (C2, W2, D2, F2)]
        v2 = [V2[d, 8:32, :] + H2[8:32, :] for d in range(2)]
        for _ in range(2):
            v2 = sweep(v2, f2, c2, w2, big2)
        down = jnp.where(lane24 < 96, 32 + half, half - 32)
        for d in range(2):
            up = pick(v2[d], down)
            H1[d, pl.ds(0, 24, stride=2), :] = up
            H1[d, pl.ds(1, 24, stride=2), :] = up

        arrive(to_mid)

        def keep_1(g, d, a, b):
            F1[d, 8 * g : 8 * g + 8, :] = a
            V1[d, 8 * g : 8 * g + 8, :] = b * masks[g]

        mid_whole(E2.at[cycle], R2.at[cycle], keep_1)
        c1, w1, big1, f1 = load(C1, 4), load(W1, 4), load(D1, 4), load(F1, 4)
        v1 = [V1[d] + H1[d // 2, 16:40, :] for d in range(4)]
        for _ in range(2):
            v1 = sweep(v1, f1, c1, w1, big1)
        for d in range(8):
            T[0, pl.ds(d, 24, stride=8), :] = v1[d // 2]

        near = lane // 2
        for q in range((9 - wide) // 2 + 2, (30 + wide) // 2 + 3):
            row = T[0, 8 * q : 8 * q + 8, :]
            up = [pick(row, near), pick(row, 64 + near)]
            for r in (2 * q - 4, 2 * q - 3):
                for t in range(2):
                    VA[t, r] = VB[t, r] + up[t]
        fine_sweep(source, rows_of(VA), 10 - wide, 30 + wide, put(VB))

        def add(t, q, v):
            K[t, q] = v if cycle == 0 else K[t, q] + v

        fine_sweep(source, rows_of(VB), 11 - wide, 29 + wide, add)

        def keep_residual(q, spread, flux):
            if final:
                v = K[0, q]
                out[pl.ds(q - OWN, DEPTH, stride=WIDE), :] = v
                res[pl.ds(q - OWN, DEPTH, stride=WIDE), :] = fine_change(q, 0, v, F.at[0], spread, flux)
            else:
                for t in range(2):
                    F[cycle + 1, t, q] = fine_change(q, t, K[t, q], F.at[0], spread, flux)

        blur_rows(rows_of(K), 12 - wide, 28 + wide, keep_residual)

    for c in ends:
        c.wait_send()


def per_device(gx_count, gy_count, rhs, cond_class, charge_class, cond_table, charge_table):
    flat = (DEPTH * WIDE, LONG)
    f32, i32 = jnp.float32, jnp.int32
    tile = (8, 128)
    fine = pltpu.VMEM((2, 40) + tile, f32)
    mid = pltpu.VMEM((4, 24, 128), f32)
    low = pltpu.VMEM((2, 48, 128), f32)
    scratch = [
        pltpu.VMEM(flat, f32), pltpu.VMEM(flat, i32), pltpu.VMEM(flat, i32), pltpu.SMEM((16,), f32), pltpu.SMEM((16,), f32),
        fine, fine, fine, pltpu.VMEM((CYCLES, 2, 40) + tile, f32), fine, fine, fine,
        pltpu.VMEM((2, 4) + tile, f32), pltpu.VMEM((2, 2, 10) + tile, f32), pltpu.VMEM((2, 192, 128), f32),
        mid, mid, mid, mid, mid,
        pltpu.VMEM((2,) + tile, f32), pltpu.VMEM((8, 2) + tile, f32),
        pltpu.VMEM((CYCLES, 4) + tile, f32), pltpu.VMEM((CYCLES, 8, 4) + tile, f32),
        pltpu.VMEM((2, 32, 128), f32), pltpu.VMEM((2, 16, 128), f32),
        pltpu.VMEM((2,) + tile, f32), pltpu.VMEM((2, 128), f32),
        pltpu.VMEM((len(AROUND),) + tile, f32), pltpu.VMEM((len(NEARER), 2, 128), f32),
        low, low, low, low, low, pltpu.VMEM((48, 128), f32),
        pltpu.VMEM((48, 128), f32), pltpu.VMEM((2, 48, 128), f32), pltpu.VMEM((3, 24, 128), f32),
        pltpu.SemaphoreType.DMA((COPIES,)), pltpu.SemaphoreType.DMA((COPIES,)), pltpu.SemaphoreType.DMA((5,)),
    ]
    hbm, vmem = pl.BlockSpec(memory_space=pl.ANY), pl.BlockSpec(memory_space=pltpu.VMEM)
    correction, residual = pl.pallas_call(
        functools.partial(kernel, gx_count, gy_count),
        out_shape=[pltpu.VMEM(flat, f32)] * 2,
        in_specs=[hbm] * 5,
        out_specs=[vmem, vmem],
        scratch_shapes=scratch,
        compiler_params=pltpu.CompilerParams(collective_id=0, has_side_effects=True),
    )(rhs.reshape(flat), cond_class.reshape(flat), charge_class.reshape(flat), cond_table, charge_table)
    return correction.reshape(rhs.shape), residual.reshape(rhs.shape)


def solution(mesh):
    placed = (P(None, "gx", "gy"), P(None, "gx", "gy"), P(None, "gx", "gy"), P(), P())
    return jax.shard_map(
        functools.partial(per_device, mesh.shape["gx"], mesh.shape["gy"]),
        mesh=mesh,
        in_specs=placed,
        out_specs=(P(None, "gx", "gy"), P(None, "gx", "gy")),
        check_vma=False,
    )
```
